512 devices in a mesh: frame: 64 (over x, z_hi, y), row: 8 (over z_lo, core).
Axes of the slice: x: 4, y: 8, z: 8 (z_hi: 2, z_lo: 4; z = z_hi * 4 + z_lo), core: 2. Of those that a mesh axis runs over, the one named last changes fastest.
Arguments:
- latents: bfloat16 [256, 32, 32, 320], P('frame', 'row'), may hold values from -20 to 20
- ln_gain: bfloat16 [320], replicated, may hold values from 0.099609375 to 1.8984375
- q_weight: bfloat16 [320, 320], replicated, may hold values from -0.30078125 to 0.30078125
- k_weight: bfloat16 [320, 320], replicated, may hold values from -3 to 3
- v_weight: bfloat16 [320, 320], replicated, may hold values from -0.3125 to 0.3125
- o_weight: bfloat16 [320, 320], replicated, may hold values from -0.3125 to 0.3125
- gn_gain: bfloat16 [320], replicated, may hold values from 0.099609375 to 1.8984375
- conv_weight: bfloat16 [3, 3, 320, 320], replicated, may hold values from -0.109375 to 0.109375
- conv_bias: bfloat16 [320], replicated, may hold values from -3 to 3
Outputs:
- output: bfloat16 [256, 32, 32, 320], P('frame', 'row')
The draws below stay inside these ranges and needn't reach their ends.
All inputs are finite; a program needn't handle non-finite values.
Results may differ from the reference program's by a relative error of at most 0.0085.
The reference program's roundings to bfloat16 on the way count: a program that leaves them out, or rounds other values in their place, can miss the bound.
Values may be sent and summed in bfloat16 or wider, within the bound.
A program may use at most 64 MiB of HBM per device.

```python
import math
import jax
import jax.numpy as jnp
from jax import lax

D = 320
HEADS = 8
GROUPS = 32
ROWS = 32
COLS = 32
FRAMES = 256


weight_edge = 0.30078125


def draw_latents(key, part):
    full_shape = (FRAMES, ROWS, COLS, D)
    keys_list = jax.random.split(key, 3)
    ramp = jnp.arange(ROWS, dtype=jnp.float32) / max(ROWS - 1, 1)
    jitter = jax.random.uniform(keys_list[1], (FRAMES, ROWS, 1, 1), minval=-0.25, maxval=0.25)
    spread = jnp.exp(math.log(3.0) * ramp[None, :, None, None] + jitter)
    rough = jnp.exp(jax.random.uniform(keys_list[2], (FRAMES, ROWS, COLS, 1), minval=-0.5, maxval=0.5))
    values = jax.random.normal(keys_list[0], full_shape) * spread * rough
    return jnp.clip(values, -20.0, 20.0).astype(jnp.bfloat16)


def shared_base(key):
    return jax.random.normal(jax.random.fold_in(key, 11), (D, D)) * math.sqrt(2.0 / D)


def draw_q_weight(key, part):
    return jnp.clip(shared_base(key), -weight_edge, weight_edge).astype(jnp.bfloat16)


def draw_k_weight(key, part):
    own_part = jax.random.normal(jax.random.fold_in(key, 12), (D, D)) * math.sqrt(2.0 / D)
    values = jnp.clip(own_part, -weight_edge, weight_edge)
    return values.astype(jnp.bfloat16)


def bell_draw(stream_key, dims, width, most, held_as=jnp.bfloat16):
    return jnp.clip(width * jax.random.normal(stream_key, dims, jnp.float32), -most, most).astype(held_as)


def setup_inputs(seed: int = 0) -> dict:
    streams_of = jax.random.split(jax.random.key(seed), 10)
    return {
        "latents": draw_latents(jax.random.fold_in(streams_of[9], 71), 0),
        "ln_gain": jnp.clip(1.0 + 0.18 * jax.random.normal(streams_of[1], (D,), jnp.float32), 0.099609375, 1.8984375).astype(jnp.bfloat16),
        "q_weight": draw_q_weight(jax.random.fold_in(streams_of[9], 71), 0),
        "k_weight": draw_k_weight(jax.random.fold_in(streams_of[9], 71), 0),
        "v_weight": bell_draw(streams_of[4], (D, D), D ** -0.5, 0.3125),
        "o_weight": bell_draw(streams_of[5], (D, D), D ** -0.5, 0.3125),
        "gn_gain": jnp.clip(1.0 + 0.18 * jax.random.normal(streams_of[6], (D,), jnp.float32), 0.099609375, 1.8984375).astype(jnp.bfloat16),
        "conv_weight": bell_draw(streams_of[7], (3, 3, D, D), (9 * D) ** -0.5, 0.109375),
        "conv_bias": bell_draw(streams_of[8], (D,), 0.5, 3.0),
    }


def layer_normed(values, gain_vec):
    floated = values.astype(jnp.float32)
    centre = floated - lax.optimization_barrier(jnp.mean(floated, axis=-1, keepdims=True))
    spread = lax.optimization_barrier(jnp.mean(centre * centre, axis=-1, keepdims=True))
    return (centre * lax.rsqrt(spread + 1e-05) * gain_vec.astype(jnp.float32)).astype(jnp.bfloat16)

def reference(latents, ln_gain, q_weight, k_weight, v_weight, o_weight, gn_gain, conv_weight, conv_bias):
    frame_tokens = ROWS * COLS
    head_dim = D // HEADS
    factor = 1.0 / math.sqrt(head_dim)
    tokens = latents.reshape(FRAMES * frame_tokens, D)
    normed = layer_normed(tokens, ln_gain)
    queries = jnp.dot(normed, q_weight, preferred_element_type=jnp.float32).astype(jnp.bfloat16)
    key_rows = jnp.dot(normed, k_weight, preferred_element_type=jnp.float32).astype(jnp.bfloat16)
    value_rows = jnp.dot(normed, v_weight, preferred_element_type=jnp.float32).astype(jnp.bfloat16)
    queries, key_rows, value_rows = lax.optimization_barrier((queries, key_rows, value_rows))
    four_shape = (FRAMES, frame_tokens, HEADS, head_dim)
    queries = queries.reshape(four_shape)
    key_rows = key_rows.reshape(four_shape)
    value_rows = value_rows.reshape(four_shape)
    earlier = jnp.maximum(jnp.arange(FRAMES, dtype=jnp.int32) - 1, 0)

    def single(index):
        frame_queries = queries[index].astype(jnp.float32)
        all_keys = jnp.concatenate([key_rows[0], key_rows[earlier[index]]], axis=0).astype(jnp.float32)
        all_values = jnp.concatenate([value_rows[0], value_rows[earlier[index]]], axis=0).astype(jnp.float32)
        scores = jnp.einsum('qhd,khd->hqk', frame_queries, all_keys) * factor
        highest = lax.optimization_barrier(jnp.max(scores, axis=-1, keepdims=True))
        raised = jnp.exp(scores - highest)
        totals = lax.optimization_barrier(jnp.sum(raised, axis=-1))
        weights = lax.optimization_barrier(raised.astype(jnp.bfloat16)).astype(jnp.float32)
        summed = jnp.einsum('hqk,khd->qhd', weights, all_values)
        return (summed / jnp.transpose(totals)[:, :, None]).astype(jnp.bfloat16)
    attended = lax.map(single, jnp.arange(FRAMES, dtype=jnp.int32)).reshape(FRAMES * frame_tokens, D)
    mixed = jnp.dot(attended, o_weight, preferred_element_type=jnp.float32)
    updated = (tokens.astype(jnp.float32) + mixed).astype(jnp.bfloat16)
    group_width = D // GROUPS
    grouped = updated.astype(jnp.float32).reshape(FRAMES, frame_tokens, GROUPS, group_width)
    counted = frame_tokens * group_width
    group_mean = lax.optimization_barrier(jnp.sum(grouped, axis=(1, 3))) / counted
    group_var = lax.optimization_barrier(jnp.sum(grouped * grouped, axis=(1, 3))) / counted - group_mean * group_mean
    scaled = (grouped - group_mean[:, None, :, None]) * lax.rsqrt(group_var + 1e-05)[:, None, :, None]
    activated = jax.nn.silu(scaled.reshape(FRAMES, frame_tokens, D) * gn_gain.astype(jnp.float32))
    activated = activated.astype(jnp.bfloat16).reshape(FRAMES, ROWS, COLS, D)
    padded = jnp.pad(activated, ((0, 0), (1, 1), (1, 1), (0, 0)))
    convolved = jnp.zeros((FRAMES * frame_tokens, D), jnp.float32)
    for row_off in range(3):
        for col_off in range(3):
            window = padded[:, row_off:row_off + ROWS, col_off:col_off + COLS, :].reshape(FRAMES * frame_tokens, D)
            convolved = convolved + jnp.dot(window, conv_weight[row_off, col_off], preferred_element_type=jnp.float32)
    output = updated.astype(jnp.float32) + convolved + conv_bias.astype(jnp.float32)
    return output.astype(jnp.bfloat16).reshape(FRAMES, ROWS, COLS, D)
```

```python
import math

import jax
import jax.numpy as jnp
from jax import lax
from jax.sharding import PartitionSpec as P

HEADS = 8
GROUPS = 32


def spread_2(value, axis, source):
    size = lax.axis_size(axis)
    place = lax.axis_index(axis)
    reach = 1
    while reach < size:
        route = [(i, i + reach) for i in range(min(reach, size - reach))]
        got = lax.ppermute(value, axis, route)
        value = jnp.where((place >= reach) & (place < 2 * reach), got, value)
        reach *= 2
    return value


def shifted(block, axis, distance):
    devices = range(lax.axis_size(axis))
    route = [(i - distance, i) for i in devices if i - distance in devices]
    return lax.ppermute(block, axis, route)


def with_halo(value, sides, width):
    for axis, dim in sides:
        size, length = (lax.axis_size(axis), value.shape[dim])
        up = [(i, (i + 1) % size) for i in range(size - 1)]
        down = [(j, i) for i, j in up]
        last = lax.slice_in_dim(value, length - width, length, axis=dim)
        leading = lax.slice_in_dim(value, 0, width, axis=dim)
        before = lax.ppermute(last, axis, up)
        after = lax.ppermute(leading, axis, down)
        value = jnp.concatenate([before, value, after], axis=dim)
    return value


def layer_normed(values, gain_vec):
    floated = values.astype(jnp.float32)
    centre = floated - jnp.mean(floated, axis=-1, keepdims=True)
    spread = jnp.mean(centre * centre, axis=-1, keepdims=True)
    return (centre * lax.rsqrt(spread + 1e-05) * gain_vec.astype(jnp.float32)).astype(jnp.bfloat16)


def attend_frames(queries, key_set, value_set, factor):
    lead_keys = key_set[0]
    lead_values = value_set[0]

    def single(operands):
        frame_queries, frame_keys, frame_values = operands
        all_keys = jnp.concatenate([lead_keys, frame_keys], axis=0)
        all_values = jnp.concatenate([lead_values, frame_values], axis=0)
        scores = (
            jnp.einsum("qhd,khd->hqk", frame_queries, all_keys, preferred_element_type=jnp.float32)
            * factor
        )
        highest = jnp.max(scores, axis=-1, keepdims=True)
        raised = jnp.exp(scores - highest)
        totals = jnp.sum(raised, axis=-1)
        summed = jnp.einsum(
            "hqk,khd->qhd",
            raised.astype(jnp.bfloat16),
            all_values,
            preferred_element_type=jnp.float32,
        )
        return (summed / jnp.transpose(totals)[:, :, None]).astype(jnp.bfloat16)

    return lax.map(single, (queries, key_set[1:], value_set[1:]))


def body(latents, ln_gain, q_weight, k_weight, v_weight, o_weight, gn_gain, conv_weight, conv_bias):
    frames, row_count, col_count, channels = latents.shape
    tok_shard = row_count * col_count
    head_dim = channels // HEADS
    factor = 1.0 / math.sqrt(head_dim)
    tokens = latents.reshape(frames * tok_shard, channels)
    kv_weight = jnp.concatenate([k_weight, v_weight], axis=1)
    normed = layer_normed(tokens, ln_gain)
    queries = jnp.dot(normed, q_weight, preferred_element_type=jnp.float32).astype(jnp.bfloat16)
    queries = queries.reshape(frames, tok_shard, channels)
    paired = jnp.dot(normed, kv_weight, preferred_element_type=jnp.float32).astype(jnp.bfloat16)
    paired = paired.reshape(frames, tok_shard, 2 * channels)
    leading = spread_2(paired[0], "frame", 0)
    earlier = shifted(paired[frames - 1], "frame", 1)
    earlier = jnp.where(lax.axis_index("frame") == 0, paired[0], earlier)
    stacked = jnp.concatenate([leading[None], earlier[None], paired[: frames - 1]], axis=0)
    sent_queries = queries.reshape(frames, tok_shard, 1, HEADS, head_dim)
    sent_pairs = stacked.reshape(frames + 1, tok_shard, 2, HEADS, head_dim)
    got_queries, got_pairs = (
        lax.all_to_all(sent_queries, "row", split_axis=3, concat_axis=1, tiled=True),
        lax.all_to_all(sent_pairs, "row", split_axis=3, concat_axis=1, tiled=True),
    )
    head_results = attend_frames(
        got_queries[:, :, 0], got_pairs[:, :, 0], got_pairs[:, :, 1], factor
    )
    returned = lax.all_to_all(head_results, "row", split_axis=1, concat_axis=2, tiled=True)
    attended = returned.reshape(frames * tok_shard, channels)
    mixed = jnp.dot(attended, o_weight, preferred_element_type=jnp.float32)
    updated = (tokens.astype(jnp.float32) + mixed).astype(jnp.bfloat16)
    group_width = channels // GROUPS
    grouped = updated.astype(jnp.float32).reshape(frames, tok_shard, GROUPS, group_width)
    sum_parts = jnp.sum(grouped, axis=(1, 3))
    square_parts = jnp.sum(grouped * grouped, axis=(1, 3))
    group_sum, group_square = lax.psum((sum_parts, square_parts), "row")
    counted = tok_shard * lax.axis_size("row") * group_width
    group_mean = group_sum / counted
    group_var = group_square / counted - group_mean * group_mean
    scaled = (grouped - group_mean[:, None, :, None]) * lax.rsqrt(group_var + 1e-05)[
        :, None, :, None
    ]
    activated = jax.nn.silu(
        scaled.reshape(frames, tok_shard, channels) * gn_gain.astype(jnp.float32)
    )
    activated = activated.astype(jnp.bfloat16).reshape(frames, row_count, col_count, channels)
    padded = with_halo(activated, (("row", 1),), 1)
    padded = jnp.pad(padded, ((0, 0), (0, 0), (1, 1), (0, 0)))
    convolved = jnp.zeros((frames * tok_shard, channels), jnp.float32)
    for row_off in range(3):
        for col_off in range(3):
            window = padded[
                :, row_off : row_off + row_count, col_off : col_off + col_count, :
            ].reshape(frames * tok_shard, channels)
            convolved = convolved + jnp.dot(
                window, conv_weight[row_off, col_off], preferred_element_type=jnp.float32
            )
    output = updated.astype(jnp.float32) + convolved + conv_bias.astype(jnp.float32)
    return output.astype(jnp.bfloat16).reshape(frames, row_count, col_count, channels)


def solution(mesh):
    in_specs = (P("frame", "row", None, None), P(), P(), P(), P(), P(), P(), P(), P())
    out_specs = P("frame", "row", None, None)
    return jax.shard_map(body, mesh=mesh, in_specs=in_specs, out_specs=out_specs, check_vma=False)
```

```python
import math, functools
import jax, jax.numpy as jnp
from jax import lax
from jax.sharding import PartitionSpec as P
from jax.experimental import pallas as pl
from jax.experimental.pallas import tpu as pltpu

HEADS = 8
GROUPS = 32
LANES = 128
PER_TILE = 3
BF = jnp.bfloat16
F32 = jnp.float32


def spread_matrix(channels, head_dim, tiles):
    used = PER_TILE * head_dim
    row = lax.broadcasted_iota(jnp.int32, (channels, tiles * LANES), 0)
    col = lax.broadcasted_iota(jnp.int32, (channels, tiles * LANES), 1)
    inside = col % LANES
    return jnp.where((inside < used) & (row == (col // LANES) * used + inside), 1.0, 0.0).astype(BF)


def dot_nt(a, b):
    return lax.dot_general(a, b, (((1,), (1,)), ((), ())), preferred_element_type=F32)


def dot_tn(a, b):
    return lax.dot_general(a, b, (((0,), (0,)), ((), ())), preferred_element_type=F32)


def dot(a, b):
    return jnp.dot(a, b, preferred_element_type=F32)


def attention_kernel(head_dim, g_ref, n_ref, x_ref, wq_ref, wk_ref, wv_ref, wo_ref, out_ref, sum_ref,
                     wkv_s, wo_s, q_s, k_s, v_s, acc_s, top_s, att_s):
    frames, own, channels = n_ref.shape
    tiles = -(-HEADS // PER_TILE)
    wide = tiles * LANES
    used = PER_TILE * head_dim
    scale = math.log2(math.e) / math.sqrt(head_dim)
    spread = spread_matrix(channels, head_dim, tiles)
    wkv_s[:, :wide] = dot(wk_ref[...], spread).astype(BF)
    wkv_s[:, wide:] = dot(wv_ref[...], spread).astype(BF)
    wo_s[...] = dot_tn(spread, wo_ref[...]).astype(BF)
    wq = dot(wq_ref[...], spread).astype(BF)
    heads_in = [min(PER_TILE, HEADS - t * PER_TILE) for t in range(tiles)]
    lane = lax.broadcasted_iota(jnp.int32, (own, LANES), 1)
    for f in range(frames):
        q = dot(n_ref[f], wq)
        for t in range(tiles):
            part = q[:, t * LANES:(t + 1) * LANES]
            for j in range(heads_in[t]):
                kept = jnp.where((lane >= j * head_dim) & (lane < (j + 1) * head_dim), part, 0.0)
                q_s[f, t, j * own:(j + 1) * own, :] = kept.astype(BF)

    def project(slot):
        rows = 256
        count = g_ref.shape[1] // rows
        inside = lax.broadcasted_iota(jnp.int32, (rows, wide), 1) % LANES
        for i in range(count):
            both = dot(g_ref[slot, i * rows:(i + 1) * rows, :], wkv_s[...])
            k_s[i * rows:(i + 1) * rows, :] = both[:, :wide].astype(BF)
            v_s[i * rows:(i + 1) * rows, :] = jnp.where(inside >= used, 1.0, both[:, wide:]).astype(BF)

    def unit(f, t):
        rows = heads_in[t] * own
        s = dot_nt(q_s[f, t, :rows, :], k_s[:, t * LANES:(t + 1) * LANES])
        top = jnp.max(s, axis=-1, keepdims=True)
        w = jnp.exp2((s - top) * scale).astype(BF)
        return top, dot(w, v_s[:, t * LANES:(t + 1) * LANES]), rows

    def first(f, carry):
        project(f)
        for t in range(tiles):
            top, acc, rows = unit(f, t)
            acc_s[f, t, :rows, :] = acc
            top_s[f, t, :rows, :] = jnp.broadcast_to(top, (rows, LANES))
        return carry

    lax.fori_loop(0, frames, first, 0)
    project(frames)

    def second(f, carry):
        for t in range(tiles):
            top, acc, rows = unit(f, t)
            before = top_s[f, t, :rows, :]
            high = jnp.maximum(before, top)
            acc = acc * jnp.exp2((top - high) * scale) + acc_s[f, t, :rows, :] * jnp.exp2((before - high) * scale)
            acc = acc / acc[:, used:used + 1]
            whole = jnp.zeros((own, LANES), F32)
            for j in range(heads_in[t]):
                whole = jnp.where((lane >= j * head_dim) & (lane < (j + 1) * head_dim),
                                  acc[j * own:(j + 1) * own, :], whole)
            att_s[f, :, t * LANES:(t + 1) * LANES] = whole.astype(BF)
        mixed = dot(att_s[f], wo_s[...])
        updated = (x_ref[f].astype(F32) + mixed).astype(BF)
        out_ref[f] = updated
        wider = updated.astype(F32)
        sum_ref[pl.ds(f, 1), :] = jnp.sum(wider, axis=0, keepdims=True)
        sum_ref[pl.ds(frames + f, 1), :] = jnp.sum(wider * wider, axis=0, keepdims=True)
        return carry

    lax.fori_loop(0, frames, second, 0)


def attention(gathered, normed, x, wq, wk, wv, wo):
    frames, own, channels = normed.shape
    head_dim = channels // HEADS
    tiles = -(-HEADS // PER_TILE)
    wide = tiles * LANES
    keys = gathered.shape[1]
    rows = PER_TILE * own
    vm = pl.BlockSpec(memory_space=pltpu.VMEM)
    return pl.pallas_call(
        functools.partial(attention_kernel, head_dim),
        out_shape=(jax.ShapeDtypeStruct((frames, own, channels), BF),
                   jax.ShapeDtypeStruct((2 * frames, channels), F32)),
        in_specs=[vm] * 7,
        out_specs=(vm, vm),
        scratch_shapes=[
            pltpu.VMEM((channels, 2 * wide), BF),
            pltpu.VMEM((wide, channels), BF),
            pltpu.VMEM((frames, tiles, rows, LANES), BF),
            pltpu.VMEM((keys, wide), BF),
            pltpu.VMEM((keys, wide), BF),
            pltpu.VMEM((frames, tiles, rows, LANES), F32),
            pltpu.VMEM((frames, tiles, rows, LANES), F32),
            pltpu.VMEM((frames, own, wide), BF),
        ],
        compiler_params=pltpu.CompilerParams(vmem_limit_bytes=48 * 1024 * 1024),
    )(gathered, normed, x, wq, wk, wv, wo)


MESH = pl.DeviceIdType.MESH


def normalize(x, gain):
    wide = x.astype(F32)
    centre = wide - jnp.mean(wide, axis=-1, keepdims=True)
    spread = jnp.mean(centre * centre, axis=-1, keepdims=True)
    return (centre * lax.rsqrt(spread + 1e-5) * gain).astype(BF)


def tree_place(b):
    y, q = b % 8, b // 8
    x, h = q // 2, q % 2
    y_depth = jnp.where(y == 0, 0, jnp.where((y == 3) | (y == 6), 1, 2))
    x_depth = jnp.where(x == 0, 0, jnp.where(x == 2, 2, 1))
    parent = jnp.where(
        x > 0,
        jnp.where(x == 3, b - 48, b - 16),
        jnp.where(
            y > 0,
            jnp.where((y == 2) | (y == 5), b + 1, jnp.where((y == 1) | (y == 4), b - 1, b - y)),
            b - 8,
        ),
    )
    edge = x == 0
    children = [
        (edge & (h == 0) & (y == 0), b + 8),
        (edge & ((y == 0) | (y == 3) | (y == 6)), jnp.where(y == 0, b + 3, b - 1)),
        (edge & ((y == 0) | (y == 3)), jnp.where(y == 0, b + 6, b + 1)),
        (edge & (y == 0), b + 1),
        (edge & (y == 0), b + 7),
        (x <= 1, b + 16),
        (edge, b + 48),
    ]
    return h + y_depth + x_depth, parent, children


TREE_DEPTH = 6
TREE_CHILDREN = 7


class Gather:
    def __init__(self, g_ref, n_ref, recv, row_send, tree_send, prev_send):
        self.g, self.n = g_ref, n_ref
        self.recv, self.row_send, self.tree_send, self.prev_send = recv, row_send, tree_send, prev_send
        self.size = lax.axis_size("frame")
        self.chips = lax.axis_size("row") // 2
        self.b = lax.axis_index("frame")
        self.r = lax.axis_index("row")
        self.z, self.c = self.r // 2, self.r % 2
        self.other = self.r + 1 - 2 * self.c
        self.depth, self.parent, children = tree_place(self.b)
        self.children = [(cond & (to < self.size), to) for cond, to in children]
        self.slots = g_ref.shape[0]
        self.lead = self.slots - 1

    def greet(self, everyone):
        barrier = pltpu.get_barrier_semaphore()
        total = jnp.int32(0)

        def hail(cond, b, r):
            @pl.when(cond)
            def _():
                pl.semaphore_signal(barrier, inc=1, device_id=(b, r), device_id_type=MESH)
            return jnp.where(cond, 1, 0)

        b, r, size = self.b, self.r, self.size
        for d in range(1, lax.axis_size("row")):
            to = (r + d) % lax.axis_size("row")
            if everyone:
                total += hail(r >= 0, b, to)
            else:
                total += hail((to == r + 2) | (to == r - 2) | (to == self.other), b, to)
        total += hail(b > 0, b - 1, r)
        total += hail(b < size - 1, b + 1, r)
        total += hail(b > 0, self.parent, r)
        for cond, to in self.children:
            total += hail(cond, to, r)
        pl.semaphore_wait(barrier, total)

    def row_copy(self, s, chip, kind, index):
        to = [self.r + 2, self.r - 2, self.other][kind]
        shard = 2 * chip + self.c
        return pltpu.make_async_remote_copy(
            src_ref=self.g.at[s, shard], dst_ref=self.g.at[s, shard],
            send_sem=self.row_send.at[s, kind, index], recv_sem=self.recv.at[s, shard],
            device_id=(self.b, to), device_id_type=MESH)

    def arrived(self, s, shard):
        pltpu.make_async_remote_copy(
            src_ref=self.g.at[s, shard], dst_ref=self.g.at[s, shard],
            send_sem=self.row_send.at[s, 0, 0], recv_sem=self.recv.at[s, shard],
            device_id=(self.b, self.other), device_id_type=MESH).wait_recv()

    def pass_on(self, s, t, right, left):
        z, last = self.z, self.chips - 1
        if right:
            @pl.when(z < last)
            def _():
                self.row_copy(s, z - t, 0, t).start()
        if left:
            @pl.when(z > 0)
            def _():
                self.row_copy(s, z + t, 1, t).start()
        chip = z - t if right else z + t
        self.row_copy(s, chip, 2, chip).start()

    def step(self, s, t):
        z, last = self.z, self.chips - 1
        if t == 0:
            self.pass_on(s, 0, True, True)
            return

        @pl.when(z - t >= 0)
        def _():
            self.arrived(s, 2 * (z - t) + self.c)
            self.pass_on(s, t, True, False)

        @pl.when(z + t <= last)
        def _():
            self.arrived(s, 2 * (z + t) + self.c)
            self.pass_on(s, t, False, True)

    def finish(self, s):
        for chip in range(self.chips):
            self.arrived(s, 2 * chip + 1 - self.c)

    def drain(self, s):
        z, last = self.z, self.chips - 1
        for t in range(self.chips):
            @pl.when((z - t >= 0) & (z < last))
            def _():
                self.row_copy(s, z - t, 0, t).wait_send()

            @pl.when((z + t <= last) & (z > 0))
            def _():
                self.row_copy(s, z + t, 1, t).wait_send()
            self.row_copy(s, t, 2, t).wait_send()

    def prev_copy(self):
        return pltpu.make_async_remote_copy(
            src_ref=self.n.at[self.n.shape[0] - 1], dst_ref=self.g.at[0, self.r],
            send_sem=self.prev_send, recv_sem=self.recv.at[0, self.r],
            device_id=(self.b + 1, self.r), device_id_type=MESH)

    def prev_start(self):
        @pl.when(self.b < self.size - 1)
        def _():
            self.prev_copy().start()

    def prev_arrived(self):
        @pl.when(self.b > 0)
        def _():
            self.arrived(0, self.r)

    def prev_drain(self):
        @pl.when(self.b < self.size - 1)
        def _():
            self.prev_copy().wait_send()

    def tree_copy(self, index, to):
        return pltpu.make_async_remote_copy(
            src_ref=self.g.at[self.lead, self.r], dst_ref=self.g.at[self.lead, self.r],
            send_sem=self.tree_send.at[index], recv_sem=self.recv.at[self.lead, self.r],
            device_id=(to, self.r), device_id_type=MESH)

    def tree_step(self, level):
        @pl.when(self.depth == level)
        def _():
            if level > 0:
                self.arrived(self.lead, self.r)
            for index, (cond, to) in enumerate(self.children):
                @pl.when(cond)
                def _():
                    self.tree_copy(index, to).start()

    def tree_drain(self):
        for index, (cond, to) in enumerate(self.children):
            @pl.when(cond)
            def _():
                self.tree_copy(index, to).wait_send()


def gather_kernel(x_ref, gain_ref, g_ref, n_ref, recv, row_send, tree_send, prev_send):
    frames = x_ref.shape[0]
    net = Gather(g_ref, n_ref, recv, row_send, tree_send, prev_send)
    net.greet(False)
    gain = gain_ref[...].astype(F32)
    for f in range(frames):
        normed = normalize(x_ref[f], gain)
        n_ref[f] = normed
        if f + 1 < frames:
            g_ref[1 + f, net.r] = normed

    @pl.when(net.b == 0)
    def _():
        g_ref[0, net.r] = n_ref[0]
        g_ref[net.lead, net.r] = n_ref[0]

    net.tree_step(0)
    net.prev_start()
    mine = list(range(1, frames))
    for s in mine:
        net.step(s, 0)
    net.prev_arrived()
    net.step(0, 0)
    order = mine + [0]
    for t in range(1, net.chips):
        for s in order:
            net.step(s, t)
        net.tree_step(t)
    for level in range(net.chips, TREE_DEPTH):
        net.tree_step(level)
    for t in range(net.chips):
        net.step(net.lead, t)
    for s in order + [net.lead]:
        net.finish(s)
    for s in order + [net.lead]:
        net.drain(s)
    net.prev_drain()
    net.tree_drain()


def gather(x, gain):
    frames, own, channels = x.shape
    rows = lax.axis_size("row")
    vm = pl.BlockSpec(memory_space=pltpu.VMEM)
    slots = frames + 1
    return pl.pallas_call(
        gather_kernel,
        out_shape=(jax.ShapeDtypeStruct((slots, rows, own, channels), BF),
                   jax.ShapeDtypeStruct((frames, own, channels), BF)),
        in_specs=[vm] * 2,
        out_specs=(vm, vm),
        scratch_shapes=[
            pltpu.SemaphoreType.DMA((slots, rows)),
            pltpu.SemaphoreType.DMA((slots, 3, rows // 2)),
            pltpu.SemaphoreType.DMA((TREE_CHILDREN,)),
            pltpu.SemaphoreType.DMA,
        ],
        compiler_params=pltpu.CompilerParams(
            collective_id=0, has_side_effects=True, vmem_limit_bytes=32 * 1024 * 1024),
    )(x, gain)


class Tail:
    def __init__(self, u_ref, all_ref, halo_ref, sum_send, sum_recv, halo_send, halo_recv):
        self.u, self.all, self.halo = u_ref, all_ref, halo_ref
        self.sum_send, self.sum_recv, self.halo_send, self.halo_recv = sum_send, sum_recv, halo_send, halo_recv
        self.rows = lax.axis_size("row")
        self.b, self.r = lax.axis_index("frame"), lax.axis_index("row")

    def peer(self, d):
        return (self.r + d) % self.rows

    def greet(self):
        barrier = pltpu.get_barrier_semaphore()
        for d in range(1, self.rows):
            pl.semaphore_signal(barrier, inc=1, device_id=(self.b, self.peer(d)), device_id_type=MESH)
        pl.semaphore_wait(barrier, self.rows - 1)

    def sum_copy(self, d):
        return pltpu.make_async_remote_copy(
            src_ref=self.all.at[0], dst_ref=self.all.at[d],
            send_sem=self.sum_send.at[d], recv_sem=self.sum_recv.at[d],
            device_id=(self.b, self.peer(d)), device_id_type=MESH)

    def halo_copy(self, side):
        width, own = self.halo.shape[2], self.u.shape[1]
        to = self.r + 1 if side == 0 else self.r - 1
        start = own - width if side == 0 else 0
        return pltpu.make_async_remote_copy(
            src_ref=self.u.at[:, pl.ds(start, width), :], dst_ref=self.halo.at[side],
            send_sem=self.halo_send.at[side], recv_sem=self.halo_recv.at[side],
            device_id=(self.b, to), device_id_type=MESH)

    def start(self):
        last = self.rows - 1

        @pl.when(self.r < last)
        def _():
            self.halo_copy(0).start()

        @pl.when(self.r > 0)
        def _():
            self.halo_copy(1).start()
        for d in range(1, self.rows):
            self.sum_copy(d).start()

    def wait(self):
        last = self.rows - 1
        for d in range(1, self.rows):
            self.sum_copy(d).wait()

        @pl.when(self.r > 0)
        def _():
            self.halo_copy(0).wait_recv()

        @pl.when(self.r < last)
        def _():
            self.halo_copy(1).wait_recv()

        @pl.when(self.r < last)
        def _():
            self.halo_copy(0).wait_send()

        @pl.when(self.r > 0)
        def _():
            self.halo_copy(1).wait_send()


def convolve(tail, gain_ref, w_ref, bias_ref, out_ref, act_s):
    u_ref, all_ref, halo_ref = tail.u, tail.all, tail.halo
    frames, own, channels = u_ref.shape
    width = halo_ref.shape[2]
    group = channels // GROUPS
    total = all_ref[0]
    for d in range(1, tail.rows):
        total = total + all_ref[d]
    same = (lax.broadcasted_iota(jnp.int32, (channels, channels), 0) // group
            == lax.broadcasted_iota(jnp.int32, (channels, channels), 1) // group)
    grouped = jnp.dot(total, jnp.where(same, 1.0, 0.0), preferred_element_type=F32,
                      precision=lax.Precision.HIGHEST)
    counted = own * tail.rows * group
    mean = grouped[:frames] / counted
    var = grouped[frames:] / counted - mean * mean
    scale = lax.rsqrt(var + 1e-5)
    gain = gain_ref[...].astype(F32)
    tall = own + 2 * width
    place = lax.broadcasted_iota(jnp.int32, (tall, channels), 0)
    column = place % width
    real = ((place >= width) | (tail.r > 0)) & ((place < width + own) | (tail.r < tail.rows - 1))
    for f in range(frames):
        u = jnp.concatenate([halo_ref[0, f], u_ref[f], halo_ref[1, f]], axis=0).astype(F32)
        v = (u - mean[f:f + 1]) * scale[f:f + 1] * gain
        v = jnp.where(real, v / (1.0 + jnp.exp(-v)), 0.0)
        act_s[0, f] = jnp.where(column == 0, 0.0, pltpu.roll(v, 1, 0)).astype(BF)
        act_s[1, f] = v.astype(BF)
        act_s[2, f] = jnp.where(column == width - 1, 0.0, pltpu.roll(v, tall - 1, 0)).astype(BF)
    total = u_ref[...].reshape(frames * own, channels).astype(F32) + bias_ref[...].astype(F32)
    summed = None
    for a in range(3):
        for b in range(3):
            window = act_s[b, :, a * width:a * width + own, :].reshape(frames * own, channels)
            part = dot(window, w_ref[a, b])
            summed = part if summed is None else summed + part
    out_ref[...] = (total + summed).astype(BF).reshape(frames, own, channels)


def tail_kernel(u_ref, sum_ref, gain_ref, w_ref, bias_ref, out_ref, all_s, halo_s, act_s,
                sum_send, sum_recv, halo_send, halo_recv):
    tail = Tail(u_ref, all_s, halo_s, sum_send, sum_recv, halo_send, halo_recv)
    all_s[0] = sum_ref[...]
    halo_r = tail.r

    @pl.when(halo_r == 0)
    def _():
        halo_s[0] = jnp.zeros(halo_s.shape[1:], BF)

    @pl.when(halo_r == tail.rows - 1)
    def _():
        halo_s[1] = jnp.zeros(halo_s.shape[1:], BF)
    tail.greet()
    tail.start()
    tail.wait()
    convolve(tail, gain_ref, w_ref, bias_ref, out_ref, act_s)


def finish(updated, sums, gain, conv, bias, width):
    frames, own, channels = updated.shape
    rows = lax.axis_size("row")
    vm = pl.BlockSpec(memory_space=pltpu.VMEM)
    return pl.pallas_call(
        tail_kernel,
        out_shape=jax.ShapeDtypeStruct((frames, own, channels), BF),
        in_specs=[vm] * 5,
        out_specs=vm,
        scratch_shapes=[
            pltpu.VMEM((rows, 2 * frames, channels), F32),
            pltpu.VMEM((2, frames, width, channels), BF),
            pltpu.VMEM((3, frames, own + 2 * width, channels), BF),
            pltpu.SemaphoreType.DMA((rows,)),
            pltpu.SemaphoreType.DMA((rows,)),
            pltpu.SemaphoreType.DMA((2,)),
            pltpu.SemaphoreType.DMA((2,)),
        ],
        compiler_params=pltpu.CompilerParams(
            collective_id=1, has_side_effects=True, vmem_limit_bytes=32 * 1024 * 1024),
    )(updated, sums, gain, conv, bias)


def body(latents, ln_gain, q_weight, k_weight, v_weight, o_weight, gn_gain, conv_weight, conv_bias):
    frames, row_count, col_count, channels = latents.shape
    x = latents.reshape(frames, row_count * col_count, channels)
    gathered, normed = gather(x, ln_gain.reshape(1, channels))
    gathered = gathered.reshape(frames + 1, -1, channels)
    updated, sums = attention(gathered, normed, x, q_weight, k_weight, v_weight, o_weight)
    out = finish(updated, sums, gn_gain.reshape(1, channels), conv_weight,
                 conv_bias.reshape(1, channels), col_count)
    return out.reshape(frames, row_count, col_count, channels)


def solution(mesh):
    in_specs = (P("frame", "row", None, None), P(), P(), P(), P(), P(), P(), P(), P())
    out_specs = P("frame", "row", None, None)
    return jax.shard_map(body, mesh=mesh, in_specs=in_specs, out_specs=out_specs, check_vma=False)
```

```python
import functools
import math

import jax
import jax.numpy as jnp
from jax import lax
from jax.experimental import pallas as pl
from jax.experimental.pallas import tpu as pltpu
from jax.sharding import PartitionSpec as P

HEADS = 8
GROUPS = 32
LANES = 128
PER_TILE = 3
BF = jnp.bfloat16
F32 = jnp.float32
MESH = pl.DeviceIdType.MESH
TREE_DEPTH = 6
TREE_CHILDREN = 7


def dot(a, b):
    return jnp.dot(a, b, preferred_element_type=F32)


def dot_nt(a, b):
    return lax.dot_general(a, b, (((1,), (1,)), ((), ())), preferred_element_type=F32)


def dot_tn(a, b):
    return lax.dot_general(a, b, (((0,), (0,)), ((), ())), preferred_element_type=F32)


def one_hot(rows, columns, test):
    row = lax.broadcasted_iota(jnp.int32, (rows, columns), 0)
    col = lax.broadcasted_iota(jnp.int32, (rows, columns), 1)
    return jnp.where(test(row, col), 1.0, 0.0).astype(BF)


def normalize(x, gain):
    wide = x.astype(F32)
    centre = wide - jnp.mean(wide, axis=-1, keepdims=True)
    spread = jnp.mean(centre * centre, axis=-1, keepdims=True)
    return (centre * lax.rsqrt(spread + 1e-5) * gain).astype(BF)


def tree_place(b):
    y, q = b % 8, b // 8
    x, h = q // 2, q % 2
    y_depth = jnp.where(y == 0, 0, jnp.where((y == 3) | (y == 6), 1, 2))
    x_depth = jnp.where(x == 0, 0, jnp.where(x == 2, 2, 1))
    y_parent = jnp.where((y == 2) | (y == 5), b + 1, jnp.where((y == 1) | (y == 4), b - 1, b - y))
    parent = jnp.where(x > 0, jnp.where(x == 3, b - 48, b - 16), jnp.where(y > 0, y_parent, b - 8))
    y_index = jnp.where((y == 1) | (y == 7), jnp.where(y == 1, 3, 4), jnp.where((y == 6) | (y == 4), 2, 1))
    index = jnp.where(x > 0, jnp.where(x == 3, 6, 5), jnp.where(y > 0, y_index, 0))
    edge = x == 0
    children = [
        (edge & (h == 0) & (y == 0), b + 8),
        (edge & ((y == 0) | (y == 3) | (y == 6)), jnp.where(y == 0, b + 3, b - 1)),
        (edge & ((y == 0) | (y == 3)), jnp.where(y == 0, b + 6, b + 1)),
        (edge & (y == 0), b + 1),
        (edge & (y == 0), b + 7),
        (x <= 1, b + 16),
        (edge, b + 48),
    ]
    return h + y_depth + x_depth, parent, index, children


TREE_ORDER = (1, 2, 3, 4, 5, 6, 0)


class Net:
    def __init__(self, g_ref, last_ref, u_ref, all_ref, halo_ref, sems):
        self.g, self.last, self.u, self.all, self.halo = g_ref, last_ref, u_ref, all_ref, halo_ref
        (self.recv, self.row_send, self.tree_send, self.prev_send, self.tree_ready, self.prev_ready,
         self.sum_send, self.sum_recv, self.halo_send, self.halo_recv) = sems
        self.size = lax.axis_size("frame")
        self.rows = lax.axis_size("row")
        self.chips = self.rows // 2
        self.b = lax.axis_index("frame")
        self.r = lax.axis_index("row")
        self.z, self.c = self.r // 2, self.r % 2
        self.other = self.r + 1 - 2 * self.c
        self.depth, self.parent, self.index, children = tree_place(self.b)
        self.children = [(cond & (to < self.size), to) for cond, to in children]
        self.lead = g_ref.shape[0] - 1

    def peer(self, d):
        return (self.r + d) % self.rows

    def hail(self):
        barrier = pltpu.get_barrier_semaphore()

        def signal(cond, b, r):
            @pl.when(cond)
            def _():
                pl.semaphore_signal(barrier, inc=1, device_id=(b, r), device_id_type=MESH)

        for d in range(1, self.rows):
            pl.semaphore_signal(barrier, inc=1, device_id=(self.b, self.peer(d)), device_id_type=MESH)
        signal(self.b < self.size - 1, self.b + 1, self.r)
        for cond, to in self.children:
            signal(cond, to, self.r)

    def greet(self):
        barrier = pltpu.get_barrier_semaphore()
        pl.semaphore_wait(barrier, self.rows - 1 + jnp.where(self.b > 0, 2, 0))

        @pl.when(self.b > 0)
        def _():
            pl.semaphore_signal(self.prev_ready, inc=1, device_id=(self.b - 1, self.r), device_id_type=MESH)
            pl.semaphore_signal(self.tree_ready.at[self.index], inc=1, device_id=(self.parent, self.r),
                                device_id_type=MESH)

    def row_copy(self, s, chip, kind, index):
        to = [self.r + 2, self.r - 2, self.other][kind]
        shard = 2 * chip + self.c
        return pltpu.make_async_remote_copy(
            src_ref=self.g.at[s, shard], dst_ref=self.g.at[s, shard],
            send_sem=self.row_send.at[s, kind, index], recv_sem=self.recv.at[s, shard],
            device_id=(self.b, to), device_id_type=MESH)

    def arrived(self, s, shard):
        pltpu.make_async_remote_copy(
            src_ref=self.g.at[s, shard], dst_ref=self.g.at[s, shard],
            send_sem=self.row_send.at[s, 0, 0], recv_sem=self.recv.at[s, shard],
            device_id=(self.b, self.other), device_id_type=MESH).wait_recv()

    def pass_on(self, s, t, right, left):
        z, last = self.z, self.chips - 1
        if right:
            @pl.when(z < last)
            def _():
                self.row_copy(s, z - t, 0, t).start()
        if left:
            @pl.when(z > 0)
            def _():
                self.row_copy(s, z + t, 1, t).start()
        chip = z - t if right else z + t
        self.row_copy(s, chip, 2, chip).start()

    def step(self, s, t):
        z, last = self.z, self.chips - 1
        if t == 0:
            self.pass_on(s, 0, True, True)
            return

        @pl.when(z - t >= 0)
        def _():
            self.arrived(s, 2 * (z - t) + self.c)
            self.pass_on(s, t, True, False)

        @pl.when(z + t <= last)
        def _():
            self.arrived(s, 2 * (z + t) + self.c)
            self.pass_on(s, t, False, True)

    def finish(self, s):
        for chip in range(self.chips):
            self.arrived(s, 2 * chip + 1 - self.c)

    def drain(self, s):
        z, last = self.z, self.chips - 1
        for t in range(self.chips):
            @pl.when((z - t >= 0) & (z < last))
            def _():
                self.row_copy(s, z - t, 0, t).wait_send()

            @pl.when((z + t <= last) & (z > 0))
            def _():
                self.row_copy(s, z + t, 1, t).wait_send()
            self.row_copy(s, t, 2, t).wait_send()

    def prev_copy(self):
        return pltpu.make_async_remote_copy(
            src_ref=self.last, dst_ref=self.g.at[0, self.r],
            send_sem=self.prev_send, recv_sem=self.recv.at[0, self.r],
            device_id=(self.b + 1, self.r), device_id_type=MESH)

    def prev_start(self):
        @pl.when(self.b < self.size - 1)
        def _():
            pl.semaphore_wait(self.prev_ready, 1)
            self.prev_copy().start()

    def prev_arrived(self):
        @pl.when(self.b > 0)
        def _():
            self.arrived(0, self.r)

    def prev_drain(self):
        @pl.when(self.b < self.size - 1)
        def _():
            self.prev_copy().wait_send()

    def tree_copy(self, index, to):
        return pltpu.make_async_remote_copy(
            src_ref=self.g.at[self.lead, self.r], dst_ref=self.g.at[self.lead, self.r],
            send_sem=self.tree_send.at[index], recv_sem=self.recv.at[self.lead, self.r],
            device_id=(to, self.r), device_id_type=MESH)

    def tree_step(self, level):
        @pl.when(self.depth == level)
        def _():
            if level > 0:
                self.arrived(self.lead, self.r)
            for index in TREE_ORDER[:-1]:
                cond, to = self.children[index]

                @pl.when(cond)
                def _():
                    pl.semaphore_wait(self.tree_ready.at[index], 1)
                    self.tree_copy(index, to).start()

    def root_step(self):
        cond, to = self.children[0]

        @pl.when(cond)
        def _():
            pl.semaphore_wait(self.tree_ready.at[0], 1)
            self.tree_copy(0, to).start()

    def tree_drain(self):
        for index, (cond, to) in enumerate(self.children):
            @pl.when(cond)
            def _():
                self.tree_copy(index, to).wait_send()

    def sum_copy(self, f, d):
        return pltpu.make_async_remote_copy(
            src_ref=self.all.at[0, f], dst_ref=self.all.at[d, f],
            send_sem=self.sum_send.at[f, d], recv_sem=self.sum_recv.at[f, d],
            device_id=(self.b, self.peer(d)), device_id_type=MESH)

    def halo_copy(self, f, side):
        width, own = self.halo.shape[2], self.u.shape[1]
        to = self.r + 1 if side == 0 else self.r - 1
        start = own - width if side == 0 else 0
        return pltpu.make_async_remote_copy(
            src_ref=self.u.at[f, pl.ds(start, width), :], dst_ref=self.halo.at[side, f],
            send_sem=self.halo_send.at[f, side], recv_sem=self.halo_recv.at[f, side],
            device_id=(self.b, to), device_id_type=MESH)

    def edge_start(self, f):
        for d in range(1, self.rows):
            self.sum_copy(f, d).start()

        @pl.when(self.r < self.rows - 1)
        def _():
            self.halo_copy(f, 0).start()

        @pl.when(self.r > 0)
        def _():
            self.halo_copy(f, 1).start()

    def edge_wait(self, f):
        for d in range(1, self.rows):
            self.sum_copy(f, d).wait_recv()

        @pl.when(self.r > 0)
        def _():
            self.halo_copy(f, 0).wait_recv()

        @pl.when(self.r < self.rows - 1)
        def _():
            self.halo_copy(f, 1).wait_recv()

    def edge_drain(self, f):
        for d in range(1, self.rows):
            self.sum_copy(f, d).wait_send()

        @pl.when(self.r < self.rows - 1)
        def _():
            self.halo_copy(f, 0).wait_send()

        @pl.when(self.r > 0)
        def _():
            self.halo_copy(f, 1).wait_send()


def block_kernel(head_dim, width, x_hbm, ln_hbm, wq_hbm, wk_hbm, wv_hbm, wo_hbm, gn_hbm, conv_hbm, bias_hbm,
                 out_ref, x_s, ln_s, gn_s, bias_s, w_s, conv_s, n_s, g_s, last_s, wkv_s, wo_s, q_s, k_s, v_s,
                 acc_s, top_s, att_s, u_s, all_s, halo_s, act_s, load, *sems):
    frames, own, channels = x_s.shape
    half = own // 2
    tiles = -(-HEADS // PER_TILE)
    wide = tiles * LANES
    used = PER_TILE * head_dim
    cut = (channels // LANES) * LANES
    scale = math.log2(math.e) / math.sqrt(head_dim)
    net = Net(g_s, last_s, u_s, all_s, halo_s, sems)
    lead = net.lead

    loads = [(x_hbm, x_s), (ln_hbm, ln_s), (wq_hbm, w_s.at[0]), (wk_hbm, w_s.at[1]),
             (wv_hbm, w_s.at[2]), (wo_hbm, w_s.at[3]), (gn_hbm, gn_s), (bias_hbm, bias_s),
             (conv_hbm, conv_s)]
    copies = [pltpu.make_async_copy(a, b, load.at[i]) for i, (a, b) in enumerate(loads)]
    for copy in copies:
        copy.start()
    net.hail()

    heads_in = [min(PER_TILE, HEADS - t * PER_TILE) for t in range(tiles)]
    lane = lax.broadcasted_iota(jnp.int32, (own, LANES), 1)
    low = one_hot(channels, 2 * channels, lambda i, j: i == j)
    high = one_hot(channels, 2 * channels, lambda i, j: i + channels == j)
    copies[0].wait()
    copies[1].wait()
    gain = ln_s[...].astype(F32).reshape(1, channels)

    def norm(f):
        normed = normalize(x_s[f], gain)
        n_s[f] = normed
        packed = (dot(normed[:half], low) + dot(normed[half:], high)).astype(BF)
        if f + 1 < frames:
            g_s[1 + f, net.r] = packed
        else:
            last_s[...] = packed
        if f == 0:
            @pl.when(net.b == 0)
            def _():
                g_s[0, net.r] = packed
                g_s[lead, net.r] = packed

    @pl.when(net.r == 0)
    def _():
        halo_s[0] = jnp.zeros(halo_s.shape[1:], BF)

    @pl.when(net.r == net.rows - 1)
    def _():
        halo_s[1] = jnp.zeros(halo_s.shape[1:], BF)

    norm(0)
    net.greet()
    net.step(1, 0)
    net.tree_step(0)
    norm(1)
    norm(frames - 1)
    norm(2)
    net.step(1, 1)
    net.step(2, 0)
    net.prev_start()

    for i in range(2, 6):
        copies[i].wait()
    spread = one_hot(channels, wide,
                     lambda i, j: (j % LANES < used) & (i == (j // LANES) * used + j % LANES))
    wq = dot(w_s[0], spread).astype(BF)
    wkv_s[...] = jnp.zeros(wkv_s.shape, BF)
    for i in range(2):
        part = dot(w_s[1 + i], spread).astype(BF)
        wkv_s[0, :channels, i * wide:(i + 1) * wide] = part
        wkv_s[1, channels - cut:2 * channels - cut, i * wide:(i + 1) * wide] = part
    wo_s[...] = dot_tn(spread, w_s[3]).astype(BF)
    net.step(1, 2)
    net.root_step()
    net.tree_step(1)
    net.step(2, 1)
    net.step(1, 3)
    for f in range(frames):
        q = dot(n_s[f], wq)
        for t in range(tiles):
            part = q[:, t * LANES:(t + 1) * LANES]
            for j in range(heads_in[t]):
                kept = jnp.where((lane >= j * head_dim) & (lane < (j + 1) * head_dim), part, 0.0)
                q_s[f, t, j * own:(j + 1) * own, :] = kept.astype(BF)

    def project(slot):
        shards = 4
        rows = shards * half
        count = g_s.shape[1] // shards
        inside = lax.broadcasted_iota(jnp.int32, (rows, wide), 1) % LANES
        for i in range(count):
            packed = g_s[slot, i * shards:(i + 1) * shards].reshape(rows, 2 * channels)
            for side in range(2):
                view = packed[:, side * cut:side * cut + wide]
                both = dot(view, wkv_s[side])
                at = (2 * i + side) * rows
                k_s[at:at + rows, :] = both[:, :wide].astype(BF)
                v_s[at:at + rows, :] = jnp.where(inside >= used, 1.0, both[:, wide:]).astype(BF)

    def unit(f, t):
        rows = heads_in[t] * own
        s = dot_nt(q_s[f, t, :rows, :], k_s[:, t * LANES:(t + 1) * LANES])
        top = jnp.max(s, axis=-1, keepdims=True)
        w = jnp.exp2((s - top) * scale).astype(BF)
        return top, dot(w, v_s[:, t * LANES:(t + 1) * LANES]), rows

    def first(f, t):
        top, acc, rows = unit(f, t)
        acc_s[f, t, :rows, :] = acc
        top_s[f, t, :rows, :] = jnp.broadcast_to(top, (rows, LANES))

    def second(f, carry):
        for t in range(tiles):
            top, acc, rows = unit(f, t)
            before = top_s[f, t, :rows, :]
            most = jnp.maximum(before, top)
            acc = acc * jnp.exp2((top - most) * scale) + acc_s[f, t, :rows, :] * jnp.exp2((before - most) * scale)
            acc = acc / acc[:, used:used + 1]
            whole = jnp.zeros((own, LANES), F32)
            for j in range(heads_in[t]):
                whole = jnp.where((lane >= j * head_dim) & (lane < (j + 1) * head_dim),
                                  acc[j * own:(j + 1) * own, :], whole)
            att_s[:, t * LANES:(t + 1) * LANES] = whole.astype(BF)
        updated = (x_s[f].astype(F32) + dot(att_s[...], wo_s[...])).astype(BF)
        u_s[f] = updated
        wider = updated.astype(F32)
        all_s[0, f, 0:1, :] = jnp.sum(wider, axis=0, keepdims=True)
        all_s[0, f, 1:2, :] = jnp.sum(wider * wider, axis=0, keepdims=True)
        net.edge_start(f)
        return carry

    net.tree_step(2)
    net.finish(1)
    project(1)
    net.step(2, 2)
    net.step(3, 0)
    net.tree_step(3)
    first(1, 0)
    net.step(3, 1)
    first(1, 1)
    net.tree_step(4)
    net.step(2, 3)
    first(1, 2)
    net.tree_step(5)
    net.step(lead, 0)
    net.finish(2)
    project(2)
    net.step(3, 2)
    first(2, 0)
    net.step(lead, 1)
    first(2, 1)
    net.step(3, 3)
    net.prev_arrived()
    net.step(0, 0)
    first(2, 2)
    net.finish(3)
    project(3)
    net.step(lead, 2)
    first(3, 0)
    net.step(0, 1)
    first(3, 1)
    net.step(lead, 3)
    first(3, 2)
    net.step(0, 2)
    net.finish(lead)
    project(lead)
    first(0, 0)
    first(0, 1)
    first(0, 2)

    def rest(f, carry):
        @pl.when(f == 1)
        def _():
            net.step(0, 3)
        return second(f, carry)

    lax.fori_loop(1, frames, rest, 0)
    net.finish(0)
    project(0)
    second(0, 0)

    for i in range(6, len(copies)):
        copies[i].wait()
    gn_gain = gn_s[...].astype(F32).reshape(1, channels)
    bias = bias_s[...].astype(F32).reshape(1, channels)
    group = channels // GROUPS
    same = (lax.broadcasted_iota(jnp.int32, (channels, channels), 0) // group
            == lax.broadcasted_iota(jnp.int32, (channels, channels), 1) // group)
    same = jnp.where(same, 1.0, 0.0)
    tall = own + 2 * width
    place = lax.broadcasted_iota(jnp.int32, (tall, channels), 0)
    column = place % width
    real = ((place >= width) | (net.r > 0)) & ((place < width + own) | (net.r < net.rows - 1))
    counted = own * net.rows * group

    def convolve(start, count):
        for f in range(start, start + count):
            net.edge_wait(f)
            total = all_s[0, f]
            for d in range(1, net.rows):
                total = total + all_s[d, f]
            grouped = jnp.dot(jnp.concatenate([total] * 4, axis=0), same, preferred_element_type=F32,
                              precision=lax.Precision.HIGHEST)
            mean = grouped[0:1] / counted
            var = grouped[1:2] / counted - mean * mean
            u = jnp.concatenate([halo_s[0, f], u_s[f], halo_s[1, f]], axis=0).astype(F32)
            v = (u - mean) * lax.rsqrt(var + 1e-5) * gn_gain
            v = jnp.where(real, v / (1.0 + jnp.exp(-v)), 0.0)
            act_s[0, f] = jnp.where(column == 0, 0.0, pltpu.roll(v, 1, 0)).astype(BF)
            act_s[1, f] = v.astype(BF)
            act_s[2, f] = jnp.where(column == width - 1, 0.0, pltpu.roll(v, tall - 1, 0)).astype(BF)
        rows = count * own
        summed = u_s[start:start + count].reshape(rows, channels).astype(F32) + bias
        for a in range(3):
            for b in range(3):
                window = act_s[b, start:start + count, a * width:a * width + own, :].reshape(rows, channels)
                summed = summed + dot(window, conv_s[a, b])
        out_ref[start:start + count] = summed.astype(BF).reshape(count, own, channels)

    convolve(1, frames - 1)
    convolve(0, 1)

    for s in range(lead + 1):
        net.drain(s)
    net.prev_drain()
    net.tree_drain()
    for f in range(frames):
        net.edge_drain(f)


def body(latents, ln_gain, q_weight, k_weight, v_weight, o_weight, gn_gain, conv_weight, conv_bias):
    frames, row_count, col_count, channels = latents.shape
    own = row_count * col_count
    head_dim = channels // HEADS
    tiles = -(-HEADS // PER_TILE)
    wide = tiles * LANES
    rows = lax.axis_size("row")
    slots = frames + 1
    keys = rows * own
    hbm = pl.BlockSpec(memory_space=pl.ANY)
    dma = pltpu.SemaphoreType.DMA
    out = pl.pallas_call(
        functools.partial(block_kernel, head_dim, col_count),
        out_shape=jax.ShapeDtypeStruct((frames, own, channels), BF),
        in_specs=[hbm] * 9,
        out_specs=pl.BlockSpec(memory_space=pltpu.VMEM),
        scratch_shapes=[
            pltpu.VMEM((frames, own, channels), BF),
            pltpu.VMEM((channels,), BF),
            pltpu.VMEM((channels,), BF),
            pltpu.VMEM((channels,), BF),
            pltpu.VMEM((4, channels, channels), BF),
            pltpu.VMEM((3, 3, channels, channels), BF),
            pltpu.VMEM((frames, own, channels), BF),
            pltpu.VMEM((slots, rows, own // 2, 2 * channels), BF),
            pltpu.VMEM((own // 2, 2 * channels), BF),
            pltpu.VMEM((2, wide, 2 * wide), BF),
            pltpu.VMEM((wide, channels), BF),
            pltpu.VMEM((frames, tiles, PER_TILE * own, LANES), BF),
            pltpu.VMEM((keys, wide), BF),
            pltpu.VMEM((keys, wide), BF),
            pltpu.VMEM((frames, tiles, PER_TILE * own, LANES), F32),
            pltpu.VMEM((frames, tiles, PER_TILE * own, LANES), F32),
            pltpu.VMEM((own, wide), BF),
            pltpu.VMEM((frames, own, channels), BF),
            pltpu.VMEM((rows, frames, 2, channels), F32),
            pltpu.VMEM((2, frames, col_count, channels), BF),
            pltpu.VMEM((3, frames, own + 2 * col_count, channels), BF),
            dma((9,)),
            dma((slots, rows)),
            dma((slots, 3, rows // 2)),
            dma((TREE_CHILDREN,)),
            dma,
            pltpu.SemaphoreType.REGULAR((TREE_CHILDREN,)),
            pltpu.SemaphoreType.REGULAR,
            dma((frames, rows)),
            dma((frames, rows)),
            dma((frames, 2)),
            dma((frames, 2)),
        ],
        compiler_params=pltpu.CompilerParams(
            collective_id=0, has_side_effects=True, vmem_limit_bytes=56 * 1024 * 1024),
    )(latents.reshape(frames, own, channels), ln_gain, q_weight, k_weight, v_weight,
      o_weight, gn_gain, conv_weight, conv_bias)
    return out.reshape(frames, row_count, col_count, channels)


def solution(mesh):
    in_specs = (P("frame", "row", None, None), P(), P(), P(), P(), P(), P(), P(), P())
    out_specs = P("frame", "row", None, None)
    return jax.shard_map(body, mesh=mesh, in_specs=in_specs, out_specs=out_specs, check_vma=False)
```

```python
import functools
import math

import jax
import jax.numpy as jnp
from jax import lax
from jax.experimental import pallas as pl
from jax.experimental.pallas import tpu as pltpu
from jax.sharding import PartitionSpec as P

HEADS = 8
GROUPS = 32
LANES = 128
PER_TILE = 3
BF = jnp.bfloat16
F32 = jnp.float32
MESH = pl.DeviceIdType.MESH
TREE_CHILDREN = 8
TREE_ORDER = (1, 2, 5, 7, 3, 4, 6)


def dot(a, b):
    return jnp.dot(a, b, preferred_element_type=F32)


def dot_nt(a, b):
    return lax.dot_general(a, b, (((1,), (1,)), ((), ())), preferred_element_type=F32)


def dot_tn(a, b):
    return lax.dot_general(a, b, (((0,), (0,)), ((), ())), preferred_element_type=F32)


def one_hot(rows, columns, test):
    row = lax.broadcasted_iota(jnp.int32, (rows, columns), 0)
    col = lax.broadcasted_iota(jnp.int32, (rows, columns), 1)
    return jnp.where(test(row, col), 1.0, 0.0).astype(BF)


def normalize(x, gain):
    wide = x.astype(F32)
    centre = wide - jnp.mean(wide, axis=-1, keepdims=True)
    spread = jnp.mean(centre * centre, axis=-1, keepdims=True)
    return (centre * lax.rsqrt(spread + 1e-5) * gain).astype(BF)


def tree_place(b, z):
    y, q = b % 8, b // 8
    x, h = q // 2, q % 2
    turn = (x + 4 - h * z) % 4
    edge = turn == 0
    depth = jnp.where(h == 1, jnp.where(z > 0, 2, 1), 0) + jnp.where(
        y == 0, 0, jnp.where((y == 3) | (y == 6), 1, 2))
    y_parent = jnp.where((y == 2) | (y == 5), b + 1, jnp.where((y == 1) | (y == 4), b - 1, b - y))
    parent = jnp.where(edge, jnp.where(y > 0, y_parent, b - 8), (h * z * 2 + h) * 8 + y)
    y_index = jnp.where((y == 1) | (y == 7), jnp.where(y == 1, 3, 4), jnp.where((y == 6) | (y == 4), 2, 1))
    index = jnp.where(edge, jnp.where(y > 0, y_index, 0), 4 + turn)
    cross = (h == 0) & (y == 0) & (x == z)

    def over_x(k):
        return (((x + k) % 4) * 2 + h) * 8 + y

    children = [
        (cross, b + 8),
        (edge & ((y == 0) | (y == 3) | (y == 6)), jnp.where(y == 0, b + 3, b - 1)),
        (edge & ((y == 0) | (y == 3)), jnp.where(y == 0, b + 6, b + 1)),
        (edge & (y == 0), b + 1),
        (edge & (y == 0), b + 7),
        (edge, over_x(1)),
        (edge, over_x(2)),
        (edge, over_x(3)),
    ]
    return edge, cross, depth, parent, index, children


OWN, LANE, FAR, CROSS = range(4)


class Net:
    def __init__(self, g_ref, last_ref, u_ref, all_ref, halo_ref, sems):
        self.g, self.last, self.u, self.all, self.halo = g_ref, last_ref, u_ref, all_ref, halo_ref
        (self.recv, self.row_send, self.tree_send, self.prev_send, self.tree_ready, self.prev_ready,
         self.sum_send, self.sum_recv, self.halo_send, self.halo_recv) = sems
        self.size = lax.axis_size("frame")
        self.rows = lax.axis_size("row")
        self.chips = self.rows // 2
        self.b = lax.axis_index("frame")
        self.r = lax.axis_index("row")
        self.z, self.c = self.r // 2, self.r % 2
        self.other = self.r + 1 - 2 * self.c
        self.end = (self.z == 0) | (self.z == self.chips - 1)
        self.edge, self.cross, self.depth, self.parent, self.index, children = tree_place(self.b, self.z)
        self.children = [(cond & (to < self.size), to) for cond, to in children]
        self.lead = g_ref.shape[0] - 1
        self.late = self.b % 16 == 15
        self.after_late = (self.b % 16 == 0) & (self.b > 0)

    def peer(self, d):
        return (self.r + d) % self.rows

    def hail(self):
        barrier = pltpu.get_barrier_semaphore()

        def signal(cond, b, r):
            @pl.when(cond)
            def _():
                pl.semaphore_signal(barrier, inc=1, device_id=(b, r), device_id_type=MESH)

        for d in range(1, self.rows):
            pl.semaphore_signal(barrier, inc=1, device_id=(self.b, self.peer(d)), device_id_type=MESH)
        signal((self.b < self.size - 1) & jnp.logical_not(self.late), self.b + 1, self.r)
        signal(self.after_late, self.b - 1, self.r)
        for cond, to in self.children:
            signal(cond, to, self.r)

    def greet(self):
        barrier = pltpu.get_barrier_semaphore()
        early = (self.b > 0) & jnp.logical_not(self.after_late)
        others = jnp.where(self.b > 0, 1, 0) + jnp.where(early, 1, 0)
        others += jnp.where(self.late & (self.b < self.size - 1), 1, 0)
        pl.semaphore_wait(barrier, self.rows - 1 + others)

        @pl.when(early)
        def _():
            pl.semaphore_signal(self.prev_ready, inc=1, device_id=(self.b - 1, self.r), device_id_type=MESH)

        @pl.when(self.b > 0)
        def _():
            pl.semaphore_signal(self.tree_ready.at[self.index], inc=1, device_id=(self.parent, self.r),
                                device_id_type=MESH)

    def shard_copy(self, s, chip, to, kind):
        ref = self.g.at[s, self.c, chip]
        return pltpu.make_async_remote_copy(
            src_ref=ref, dst_ref=ref, send_sem=self.row_send.at[s], recv_sem=self.recv.at[s, kind],
            device_id=(self.b, to), device_id_type=MESH)

    def several(self, s, core, count, kind):
        ref = self.g.at[s, core, pl.ds(0, count)]
        return pltpu.make_async_remote_copy(
            src_ref=ref, dst_ref=ref, send_sem=self.row_send.at[s], recv_sem=self.recv.at[s, kind],
            device_id=(self.b, self.other), device_id_type=MESH)

    def spread_own(self, s):
        z, last = self.z, self.chips - 1
        two = jnp.where(self.end, FAR, LANE)
        for step in (1, 2):
            kind = LANE if step == 1 else two

            @pl.when(z + step <= last)
            def _():
                self.shard_copy(s, z, self.r + 2 * step, kind).start()

            @pl.when(z - step >= 0)
            def _():
                self.shard_copy(s, z, self.r - 2 * step, kind).start()

    def forward(self, s):
        last = self.chips - 1

        @pl.when(self.z == 1)
        def _():
            self.several(s, self.c, 1, FAR).wait_recv()
            self.shard_copy(s, last, self.r - 2, LANE).start()

        @pl.when(self.z == last - 1)
        def _():
            self.several(s, self.c, 1, FAR).wait_recv()
            self.shard_copy(s, 0, self.r + 2, LANE).start()

    def hand_over(self, s):
        @pl.when(self.end)
        def _():
            self.several(s, self.c, 3, LANE).wait_recv()

        @pl.when(jnp.logical_not(self.end))
        def _():
            self.several(s, self.c, 2, LANE).wait_recv()
        self.several(s, self.c, self.chips, CROSS).start()

    def finish(self, s):
        self.several(s, 1 - self.c, self.chips, CROSS).wait_recv()

    def drain(self, s):
        @pl.when(self.end)
        def _():
            self.several(s, self.c, 2, LANE).wait_send()

        @pl.when(jnp.logical_not(self.end))
        def _():
            self.several(s, self.c, 4, LANE).wait_send()
        self.several(s, self.c, self.chips, LANE).wait_send()

    def own_arrived(self, s):
        self.several(s, self.c, 1, OWN).wait_recv()

    def prev_copy(self):
        return pltpu.make_async_remote_copy(
            src_ref=self.last, dst_ref=self.g.at[0, self.c, self.z],
            send_sem=self.prev_send, recv_sem=self.recv.at[0, OWN],
            device_id=(self.b + 1, self.r), device_id_type=MESH)

    def prev_start(self):
        @pl.when((self.b < self.size - 1) & jnp.logical_not(self.late))
        def _():
            pl.semaphore_wait(self.prev_ready, 1)

        @pl.when(self.b < self.size - 1)
        def _():
            self.prev_copy().start()

    def prev_arrived(self):
        @pl.when(self.b > 0)
        def _():
            self.own_arrived(0)

    def prev_drain(self):
        @pl.when(self.b < self.size - 1)
        def _():
            self.prev_copy().wait_send()

    def tree_copy(self, index, to):
        ref = self.g.at[self.lead, self.c, self.z]
        return pltpu.make_async_remote_copy(
            src_ref=ref, dst_ref=ref, send_sem=self.tree_send.at[index],
            recv_sem=self.recv.at[self.lead, OWN], device_id=(to, self.r), device_id_type=MESH)

    def tree_one(self, index):
        cond, to = self.children[index]

        @pl.when(cond)
        def _():
            pl.semaphore_wait(self.tree_ready.at[index], 1)
            self.tree_copy(index, to).start()

    def tree_step(self, level):
        @pl.when(self.edge & (self.depth == level))
        def _():
            if level > 0:
                self.own_arrived(self.lead)
            for index in TREE_ORDER:
                self.tree_one(index)

    def cross_step(self):
        @pl.when(self.cross & (self.b > 0))
        def _():
            self.own_arrived(self.lead)
        self.tree_one(0)

    def lead_arrived(self):
        @pl.when(jnp.logical_not(self.edge | self.cross))
        def _():
            self.own_arrived(self.lead)

    def tree_drain(self):
        for index, (cond, to) in enumerate(self.children):
            @pl.when(cond)
            def _():
                self.tree_copy(index, to).wait_send()

    def sum_copy(self, group, d):
        a, n = group
        return pltpu.make_async_remote_copy(
            src_ref=self.all.at[0, pl.ds(a, n)], dst_ref=self.all.at[d, pl.ds(a, n)],
            send_sem=self.sum_send.at[a], recv_sem=self.sum_recv.at[a],
            device_id=(self.b, self.peer(d)), device_id_type=MESH)

    def sum_all(self, group):
        a, n = group
        ref = self.all.at[pl.ds(1, self.rows - 1), pl.ds(a, n)]
        return pltpu.make_async_remote_copy(
            src_ref=ref, dst_ref=ref, send_sem=self.sum_send.at[a], recv_sem=self.sum_recv.at[a],
            device_id=(self.b, self.other), device_id_type=MESH)

    def halo_copy(self, group, side):
        a, n = group
        width, own = self.halo.shape[2], self.u.shape[1]
        to = self.r + 1 if side == 0 else self.r - 1
        start = own - width if side == 0 else 0
        return pltpu.make_async_remote_copy(
            src_ref=self.u.at[pl.ds(a, n), pl.ds(start, width), :], dst_ref=self.halo.at[side, pl.ds(a, n)],
            send_sem=self.halo_send.at[a, side], recv_sem=self.halo_recv.at[a, side],
            device_id=(self.b, to), device_id_type=MESH)

    def edge_start(self, group):
        for d in range(1, self.rows):
            self.sum_copy(group, d).start()

        @pl.when(self.r < self.rows - 1)
        def _():
            self.halo_copy(group, 0).start()

        @pl.when(self.r > 0)
        def _():
            self.halo_copy(group, 1).start()

    def edge_wait(self, group):
        self.sum_all(group).wait_recv()

        @pl.when(self.r > 0)
        def _():
            self.halo_copy(group, 0).wait_recv()

        @pl.when(self.r < self.rows - 1)
        def _():
            self.halo_copy(group, 1).wait_recv()

    def edge_drain(self, group):
        self.sum_all(group).wait_send()

        @pl.when(self.r < self.rows - 1)
        def _():
            self.halo_copy(group, 0).wait_send()

        @pl.when(self.r > 0)
        def _():
            self.halo_copy(group, 1).wait_send()


def block_kernel(head_dim, width, x_hbm, ln_hbm, wq_hbm, wk_hbm, wv_hbm, wo_hbm, gn_hbm, conv_hbm, bias_hbm,
                 out_ref, x_s, ln_s, gn_s, bias_s, w_s, conv_s, n_s, g_s, last_s, wkv_s, wo_s, q_s, k_s, v_s,
                 acc_s, top_s, att_s, u_s, all_s, halo_s, act_s, load, *sems):
    frames, own, channels = x_s.shape
    half = own // 2
    tiles = -(-HEADS // PER_TILE)
    wide = tiles * LANES
    used = PER_TILE * head_dim
    cut = (channels // LANES) * LANES
    scale = math.log2(math.e) / math.sqrt(head_dim)
    net = Net(g_s, last_s, u_s, all_s, halo_s, sems)
    lead = net.lead

    loads = [(x_hbm, x_s), (ln_hbm, ln_s), (wq_hbm, w_s.at[0]), (wk_hbm, w_s.at[1]),
             (wv_hbm, w_s.at[2]), (wo_hbm, w_s.at[3]), (gn_hbm, gn_s), (bias_hbm, bias_s),
             (conv_hbm, conv_s)]
    copies = [pltpu.make_async_copy(a, b, load.at[i]) for i, (a, b) in enumerate(loads)]
    for copy in copies:
        copy.start()
    net.hail()

    heads_in = [min(PER_TILE, HEADS - t * PER_TILE) for t in range(tiles)]
    lane = lax.broadcasted_iota(jnp.int32, (own, LANES), 1)
    low = one_hot(channels, 2 * channels, lambda i, j: i == j)
    high = one_hot(channels, 2 * channels, lambda i, j: i + channels == j)
    copies[0].wait()
    copies[1].wait()
    gain = ln_s[...].astype(F32).reshape(1, channels)

    def norm(f):
        normed = normalize(x_s[f], gain)
        n_s[f] = normed
        packed = (dot(normed[:half], low) + dot(normed[half:], high)).astype(BF)
        if f + 1 < frames:
            g_s[1 + f, net.c, net.z] = packed
        else:
            last_s[...] = packed
        if f == 0:
            @pl.when(net.b == 0)
            def _():
                g_s[0, net.c, net.z] = packed
                g_s[lead, net.c, net.z] = packed

    @pl.when(net.r == 0)
    def _():
        halo_s[0] = jnp.zeros(halo_s.shape[1:], BF)

    @pl.when(net.r == net.rows - 1)
    def _():
        halo_s[1] = jnp.zeros(halo_s.shape[1:], BF)

    norm(0)
    net.greet()
    net.spread_own(1)
    net.tree_step(0)
    norm(1)
    net.spread_own(2)
    norm(frames - 1)
    norm(2)
    net.prev_start()

    for i in range(2, 6):
        copies[i].wait()
    spread = one_hot(channels, wide,
                     lambda i, j: (j % LANES < used) & (i == (j // LANES) * used + j % LANES))
    wq = dot(w_s[0], spread).astype(BF)
    wkv_s[...] = jnp.zeros(wkv_s.shape, BF)
    for i in range(2):
        part = dot(w_s[1 + i], spread).astype(BF)
        wkv_s[0, :channels, i * wide:(i + 1) * wide] = part
        wkv_s[1, channels - cut:2 * channels - cut, i * wide:(i + 1) * wide] = part
    wo_s[...] = dot_tn(spread, w_s[3]).astype(BF)
    net.forward(1)
    net.spread_own(3)
    net.tree_step(1)
    net.cross_step()
    for f in range(frames):
        q = dot(n_s[f], wq)
        for t in range(tiles):
            part = q[:, t * LANES:(t + 1) * LANES]
            for j in range(heads_in[t]):
                kept = jnp.where((lane >= j * head_dim) & (lane < (j + 1) * head_dim), part, 0.0)
                q_s[f, t, j * own:(j + 1) * own, :] = kept.astype(BF)

    def project(slot):
        rows = g_s.shape[2] * half
        count = g_s.shape[1]
        inside = lax.broadcasted_iota(jnp.int32, (rows, wide), 1) % LANES
        for i in range(count):
            packed = g_s[slot, i].reshape(rows, 2 * channels)
            for side in range(2):
                view = packed[:, side * cut:side * cut + wide]
                both = dot(view, wkv_s[side])
                at = (2 * i + side) * rows
                k_s[at:at + rows, :] = both[:, :wide].astype(BF)
                v_s[at:at + rows, :] = jnp.where(inside >= used, 1.0, both[:, wide:]).astype(BF)

    def unit(f, t):
        rows = heads_in[t] * own
        s = dot_nt(q_s[f, t, :rows, :], k_s[:, t * LANES:(t + 1) * LANES])
        top = jnp.max(s, axis=-1, keepdims=True)
        w = jnp.exp2((s - top) * scale).astype(BF)
        return top, dot(w, v_s[:, t * LANES:(t + 1) * LANES]), rows

    def first(f, t):
        top, acc, rows = unit(f, t)
        acc_s[f, t, :rows, :] = acc
        top_s[f, t, :rows, :] = jnp.broadcast_to(top, (rows, LANES))

    def second(f, carry):
        for t in range(tiles):
            top, acc, rows = unit(f, t)
            before = top_s[f, t, :rows, :]
            most = jnp.maximum(before, top)
            acc = acc * jnp.exp2((top - most) * scale) + acc_s[f, t, :rows, :] * jnp.exp2((before - most) * scale)
            acc = acc / acc[:, used:used + 1]
            whole = jnp.zeros((own, LANES), F32)
            for j in range(heads_in[t]):
                whole = jnp.where((lane >= j * head_dim) & (lane < (j + 1) * head_dim),
                                  acc[j * own:(j + 1) * own, :], whole)
            att_s[:, t * LANES:(t + 1) * LANES] = whole.astype(BF)
        updated = (x_s[f].astype(F32) + dot(att_s[...], wo_s[...])).astype(BF)
        u_s[f] = updated
        wider = updated.astype(F32)
        all_s[0, f, 0:1, :] = jnp.sum(wider, axis=0, keepdims=True)
        all_s[0, f, 1:2, :] = jnp.sum(wider * wider, axis=0, keepdims=True)
        return carry

    net.forward(2)
    net.hand_over(1)
    net.tree_step(2)
    net.finish(1)
    project(1)
    net.forward(3)
    first(1, 0)
    net.tree_step(3)
    net.hand_over(2)
    first(1, 1)
    net.tree_step(4)
    net.lead_arrived()
    net.spread_own(lead)
    first(1, 2)
    net.finish(2)
    project(2)
    net.prev_arrived()
    net.spread_own(0)
    first(2, 0)
    net.hand_over(3)
    first(2, 1)
    net.forward(lead)
    first(2, 2)
    net.finish(3)
    project(3)
    first(3, 0)
    net.forward(0)
    first(3, 1)
    net.hand_over(lead)
    first(3, 2)
    net.finish(lead)
    project(lead)
    first(0, 0)
    first(0, 1)
    first(0, 2)

    def rest(f, carry):
        @pl.when(f == frames - 1)
        def _():
            net.hand_over(0)
        return second(f, carry)

    lax.fori_loop(1, frames, rest, 0)
    most, final = (1, frames - 1), (0, 1)
    net.edge_start(most)
    net.finish(0)
    project(0)
    second(0, 0)
    net.edge_start(final)

    for i in range(6, len(copies)):
        copies[i].wait()
    gn_gain = gn_s[...].astype(F32).reshape(1, channels)
    bias = bias_s[...].astype(F32).reshape(1, channels)
    group = channels // GROUPS
    same = (lax.broadcasted_iota(jnp.int32, (channels, channels), 0) // group
            == lax.broadcasted_iota(jnp.int32, (channels, channels), 1) // group)
    same = jnp.where(same, 1.0, 0.0)
    tall = own + 2 * width
    place = lax.broadcasted_iota(jnp.int32, (tall, channels), 0)
    column = place % width
    real = ((place >= width) | (net.r > 0)) & ((place < width + own) | (net.r < net.rows - 1))
    counted = own * net.rows * group

    def convolve(group):
        start, count = group
        net.edge_wait(group)
        for f in range(start, start + count):
            total = all_s[0, f]
            for d in range(1, net.rows):
                total = total + all_s[d, f]
            grouped = jnp.dot(jnp.concatenate([total] * 4, axis=0), same, preferred_element_type=F32,
                              precision=lax.Precision.HIGHEST)
            mean = grouped[0:1] / counted
            var = grouped[1:2] / counted - mean * mean
            u = jnp.concatenate([halo_s[0, f], u_s[f], halo_s[1, f]], axis=0).astype(F32)
            v = (u - mean) * lax.rsqrt(var + 1e-5) * gn_gain
            v = jnp.where(real, v / (1.0 + jnp.exp(-v)), 0.0)
            act_s[0, f] = jnp.where(column == 0, 0.0, pltpu.roll(v, 1, 0)).astype(BF)
            act_s[1, f] = v.astype(BF)
            act_s[2, f] = jnp.where(column == width - 1, 0.0, pltpu.roll(v, tall - 1, 0)).astype(BF)
        rows = count * own
        summed = u_s[start:start + count].reshape(rows, channels).astype(F32) + bias
        for a in range(3):
            for b in range(3):
                window = act_s[b, start:start + count, a * width:a * width + own, :].reshape(rows, channels)
                summed = summed + dot(window, conv_s[a, b])
        out_ref[start:start + count] = summed.astype(BF).reshape(count, own, channels)

    convolve(most)
    convolve(final)

    for s in range(lead + 1):
        net.drain(s)
    net.prev_drain()
    net.tree_drain()
    net.edge_drain(most)
    net.edge_drain(final)


def body(latents, ln_gain, q_weight, k_weight, v_weight, o_weight, gn_gain, conv_weight, conv_bias):
    frames, row_count, col_count, channels = latents.shape
    own = row_count * col_count
    head_dim = channels // HEADS
    tiles = -(-HEADS // PER_TILE)
    wide = tiles * LANES
    rows = lax.axis_size("row")
    slots = frames + 1
    keys = rows * own
    hbm = pl.BlockSpec(memory_space=pl.ANY)
    dma = pltpu.SemaphoreType.DMA
    out = pl.pallas_call(
        functools.partial(block_kernel, head_dim, col_count),
        out_shape=jax.ShapeDtypeStruct((frames, own, channels), BF),
        in_specs=[hbm] * 9,
        out_specs=pl.BlockSpec(memory_space=pltpu.VMEM),
        scratch_shapes=[
            pltpu.VMEM((frames, own, channels), BF),
            pltpu.VMEM((channels,), BF),
            pltpu.VMEM((channels,), BF),
            pltpu.VMEM((channels,), BF),
            pltpu.VMEM((4, channels, channels), BF),
            pltpu.VMEM((3, 3, channels, channels), BF),
            pltpu.VMEM((frames, own, channels), BF),
            pltpu.VMEM((slots, 2, rows // 2, own // 2, 2 * channels), BF),
            pltpu.VMEM((own // 2, 2 * channels), BF),
            pltpu.VMEM((2, wide, 2 * wide), BF),
            pltpu.VMEM((wide, channels), BF),
            pltpu.VMEM((frames, tiles, PER_TILE * own, LANES), BF),
            pltpu.VMEM((keys, wide), BF),
            pltpu.VMEM((keys, wide), BF),
            pltpu.VMEM((frames, tiles, PER_TILE * own, LANES), F32),
            pltpu.VMEM((frames, tiles, PER_TILE * own, LANES), F32),
            pltpu.VMEM((own, wide), BF),
            pltpu.VMEM((frames, own, channels), BF),
            pltpu.VMEM((rows, frames, 2, channels), F32),
            pltpu.VMEM((2, frames, col_count, channels), BF),
            pltpu.VMEM((3, frames, own + 2 * col_count, channels), BF),
            dma((9,)),
            dma((slots, 4)),
            dma((slots,)),
            dma((TREE_CHILDREN,)),
            dma,
            pltpu.SemaphoreType.REGULAR((TREE_CHILDREN,)),
            pltpu.SemaphoreType.REGULAR,
            dma((frames,)),
            dma((frames,)),
            dma((frames, 2)),
            dma((frames, 2)),
        ],
        compiler_params=pltpu.CompilerParams(
            collective_id=0, has_side_effects=True, vmem_limit_bytes=56 * 1024 * 1024),
    )(latents.reshape(frames, own, channels), ln_gain, q_weight, k_weight, v_weight,
      o_weight, gn_gain, conv_weight, conv_bias)
    return out.reshape(frames, row_count, col_count, channels)


def solution(mesh):
    in_specs = (P("frame", "row", None, None), P(), P(), P(), P(), P(), P(), P(), P())
    out_specs = P("frame", "row", None, None)
    return jax.shard_map(body, mesh=mesh, in_specs=in_specs, out_specs=out_specs, check_vma=False)
```

```python
import functools
import math

import jax
import jax.numpy as jnp
from jax import lax
from jax.experimental import pallas as pl
from jax.experimental.pallas import tpu as pltpu
from jax.sharding import PartitionSpec as P

HEADS = 8
GROUPS = 32
LANES = 128
PER_TILE = 3
BF = jnp.bfloat16
F32 = jnp.float32
MESH = pl.DeviceIdType.MESH
TREE_CHILDREN = 8
TREE_ORDER = (1, 2, 5, 7, 3, 4, 6)


def dot(a, b):
    return jnp.dot(a, b, preferred_element_type=F32)


def dot_nt(a, b):
    return lax.dot_general(a, b, (((1,), (1,)), ((), ())), preferred_element_type=F32)


def dot_tn(a, b):
    return lax.dot_general(a, b, (((0,), (0,)), ((), ())), preferred_element_type=F32)


def one_hot(rows, columns, test):
    row = lax.broadcasted_iota(jnp.int32, (rows, columns), 0)
    col = lax.broadcasted_iota(jnp.int32, (rows, columns), 1)
    return jnp.where(test(row, col), 1.0, 0.0).astype(BF)


def normalize(x, gain):
    wide = x.astype(F32)
    centre = wide - jnp.mean(wide, axis=-1, keepdims=True)
    spread = jnp.mean(centre * centre, axis=-1, keepdims=True)
    return (centre * lax.rsqrt(spread + 1e-5) * gain).astype(BF)


def tree_place(b, z):
    y, q = b % 8, b // 8
    x, h = q // 2, q % 2
    turn = (x + 4 - h * z) % 4
    edge = turn == 0
    depth = jnp.where(h == 1, jnp.where(z > 0, 2, 1), 0) + jnp.where(
        y == 0, 0, jnp.where((y == 3) | (y == 6), 1, 2))
    y_parent = jnp.where((y == 2) | (y == 5), b + 1, jnp.where((y == 1) | (y == 4), b - 1, b - y))
    parent = jnp.where(edge, jnp.where(y > 0, y_parent, b - 8), (h * z * 2 + h) * 8 + y)
    y_index = jnp.where((y == 1) | (y == 7), jnp.where(y == 1, 3, 4), jnp.where((y == 6) | (y == 4), 2, 1))
    index = jnp.where(edge, jnp.where(y > 0, y_index, 0), 4 + turn)
    cross = (h == 0) & (y == 0) & (x == z)

    def over_x(k):
        return (((x + k) % 4) * 2 + h) * 8 + y

    children = [
        (cross, b + 8),
        (edge & ((y == 0) | (y == 3) | (y == 6)), jnp.where(y == 0, b + 3, b - 1)),
        (edge & ((y == 0) | (y == 3)), jnp.where(y == 0, b + 6, b + 1)),
        (edge & (y == 0), b + 1),
        (edge & (y == 0), b + 7),
        (edge, over_x(1)),
        (edge, over_x(2)),
        (edge, over_x(3)),
    ]
    return edge, cross, depth, parent, index, children


OWN, LANE, FAR, CROSS = range(4)


class Net:
    def __init__(self, g_ref, last_ref, u_ref, all_ref, halo_ref, sems):
        self.g, self.last, self.u, self.all, self.halo = g_ref, last_ref, u_ref, all_ref, halo_ref
        (self.recv, self.row_send, self.tree_send, self.prev_send, self.tree_ready, self.prev_ready,
         self.sum_send, self.sum_recv, self.halo_send, self.halo_recv) = sems
        self.size = lax.axis_size("frame")
        self.rows = lax.axis_size("row")
        self.chips = self.rows // 2
        self.b = lax.axis_index("frame")
        self.r = lax.axis_index("row")
        self.z, self.c = self.r // 2, self.r % 2
        self.other = self.r + 1 - 2 * self.c
        self.end = (self.z == 0) | (self.z == self.chips - 1)
        self.edge, self.cross, self.depth, self.parent, self.index, children = tree_place(self.b, self.z)
        self.children = [(cond & (to < self.size), to) for cond, to in children]
        self.lead = g_ref.shape[0] - 1
        self.late = self.b % 16 == 15
        self.after_late = (self.b % 16 == 0) & (self.b > 0)

    def peer(self, d):
        return (self.r + d) % self.rows

    def hail(self):
        barrier = pltpu.get_barrier_semaphore()

        def signal(cond, b, r):
            @pl.when(cond)
            def _():
                pl.semaphore_signal(barrier, inc=1, device_id=(b, r), device_id_type=MESH)

        for d in range(1, self.rows):
            pl.semaphore_signal(barrier, inc=1, device_id=(self.b, self.peer(d)), device_id_type=MESH)
        signal((self.b < self.size - 1) & jnp.logical_not(self.late), self.b + 1, self.r)
        signal(self.after_late, self.b - 1, self.r)
        for cond, to in self.children:
            signal(cond, to, self.r)

    def greet(self):
        barrier = pltpu.get_barrier_semaphore()
        early = (self.b > 0) & jnp.logical_not(self.after_late)
        others = jnp.where(self.b > 0, 1, 0) + jnp.where(early, 1, 0)
        others += jnp.where(self.late & (self.b < self.size - 1), 1, 0)
        pl.semaphore_wait(barrier, self.rows - 1 + others)

        @pl.when(early)
        def _():
            pl.semaphore_signal(self.prev_ready, inc=1, device_id=(self.b - 1, self.r), device_id_type=MESH)

        @pl.when(self.b > 0)
        def _():
            pl.semaphore_signal(self.tree_ready.at[self.index], inc=1, device_id=(self.parent, self.r),
                                device_id_type=MESH)

    def shard_copy(self, s, chip, to, kind):
        ref = self.g.at[s, self.c, chip]
        return pltpu.make_async_remote_copy(
            src_ref=ref, dst_ref=ref, send_sem=self.row_send.at[s], recv_sem=self.recv.at[s, kind],
            device_id=(self.b, to), device_id_type=MESH)

    def several(self, s, core, count, kind):
        ref = self.g.at[s, core, pl.ds(0, count)]
        return pltpu.make_async_remote_copy(
            src_ref=ref, dst_ref=ref, send_sem=self.row_send.at[s], recv_sem=self.recv.at[s, kind],
            device_id=(self.b, self.other), device_id_type=MESH)

    def spread_own(self, s):
        z, last = self.z, self.chips - 1
        two = jnp.where(self.end, FAR, LANE)
        for step in (1, 2):
            kind = LANE if step == 1 else two

            @pl.when(z + step <= last)
            def _():
                self.shard_copy(s, z, self.r + 2 * step, kind).start()

            @pl.when(z - step >= 0)
            def _():
                self.shard_copy(s, z, self.r - 2 * step, kind).start()

    def forward(self, s):
        last = self.chips - 1

        @pl.when(self.z == 1)
        def _():
            self.several(s, self.c, 1, FAR).wait_recv()
            self.shard_copy(s, last, self.r - 2, LANE).start()

        @pl.when(self.z == last - 1)
        def _():
            self.several(s, self.c, 1, FAR).wait_recv()
            self.shard_copy(s, 0, self.r + 2, LANE).start()

    def hand_over(self, s):
        @pl.when(self.end)
        def _():
            self.several(s, self.c, 3, LANE).wait_recv()

        @pl.when(jnp.logical_not(self.end))
        def _():
            self.several(s, self.c, 2, LANE).wait_recv()
        self.several(s, self.c, self.chips, CROSS).start()

    def finish(self, s):
        self.several(s, 1 - self.c, self.chips, CROSS).wait_recv()

    def drain(self, s):
        @pl.when(self.end)
        def _():
            self.several(s, self.c, 2, LANE).wait_send()

        @pl.when(jnp.logical_not(self.end))
        def _():
            self.several(s, self.c, 4, LANE).wait_send()
        self.several(s, self.c, self.chips, LANE).wait_send()

    def own_arrived(self, s):
        self.several(s, self.c, 1, OWN).wait_recv()

    def prev_copy(self):
        return pltpu.make_async_remote_copy(
            src_ref=self.last, dst_ref=self.g.at[0, self.c, self.z],
            send_sem=self.prev_send, recv_sem=self.recv.at[0, OWN],
            device_id=(self.b + 1, self.r), device_id_type=MESH)

    def prev_start(self):
        @pl.when((self.b < self.size - 1) & jnp.logical_not(self.late))
        def _():
            pl.semaphore_wait(self.prev_ready, 1)

        @pl.when(self.b < self.size - 1)
        def _():
            self.prev_copy().start()

    def prev_arrived(self):
        @pl.when(self.b > 0)
        def _():
            self.own_arrived(0)

    def prev_drain(self):
        @pl.when(self.b < self.size - 1)
        def _():
            self.prev_copy().wait_send()

    def tree_copy(self, index, to):
        ref = self.g.at[self.lead, self.c, self.z]
        return pltpu.make_async_remote_copy(
            src_ref=ref, dst_ref=ref, send_sem=self.tree_send.at[index],
            recv_sem=self.recv.at[self.lead, OWN], device_id=(to, self.r), device_id_type=MESH)

    def tree_one(self, index):
        cond, to = self.children[index]

        @pl.when(cond)
        def _():
            pl.semaphore_wait(self.tree_ready.at[index], 1)
            self.tree_copy(index, to).start()

    def tree_step(self, level):
        @pl.when(self.edge & (self.depth == level))
        def _():
            if level > 0:
                self.own_arrived(self.lead)
            for index in TREE_ORDER:
                self.tree_one(index)

    def cross_step(self):
        @pl.when(self.cross & (self.b > 0))
        def _():
            self.own_arrived(self.lead)
        self.tree_one(0)

    def lead_arrived(self):
        @pl.when(jnp.logical_not(self.edge | self.cross))
        def _():
            self.own_arrived(self.lead)

    def tree_drain(self):
        for index, (cond, to) in enumerate(self.children):
            @pl.when(cond)
            def _():
                self.tree_copy(index, to).wait_send()

    def sum_copy(self, group, d):
        a, n = group
        return pltpu.make_async_remote_copy(
            src_ref=self.all.at[0, pl.ds(a, n)], dst_ref=self.all.at[d, pl.ds(a, n)],
            send_sem=self.sum_send.at[a], recv_sem=self.sum_recv.at[a],
            device_id=(self.b, self.peer(d)), device_id_type=MESH)

    def sum_all(self, group):
        a, n = group
        ref = self.all.at[pl.ds(1, self.rows - 1), pl.ds(a, n)]
        return pltpu.make_async_remote_copy(
            src_ref=ref, dst_ref=ref, send_sem=self.sum_send.at[a], recv_sem=self.sum_recv.at[a],
            device_id=(self.b, self.other), device_id_type=MESH)

    def halo_copy(self, group, side):
        a, n = group
        width, own = self.halo.shape[2], self.u.shape[1]
        to = self.r + 1 if side == 0 else self.r - 1
        start = own - width if side == 0 else 0
        return pltpu.make_async_remote_copy(
            src_ref=self.u.at[pl.ds(a, n), pl.ds(start, width), :], dst_ref=self.halo.at[side, pl.ds(a, n)],
            send_sem=self.halo_send.at[a, side], recv_sem=self.halo_recv.at[a, side],
            device_id=(self.b, to), device_id_type=MESH)

    def edge_start(self, group):
        for d in range(1, self.rows):
            self.sum_copy(group, d).start()

        @pl.when(self.r < self.rows - 1)
        def _():
            self.halo_copy(group, 0).start()

        @pl.when(self.r > 0)
        def _():
            self.halo_copy(group, 1).start()

    def edge_wait(self, group):
        self.sum_all(group).wait_recv()

        @pl.when(self.r > 0)
        def _():
            self.halo_copy(group, 0).wait_recv()

        @pl.when(self.r < self.rows - 1)
        def _():
            self.halo_copy(group, 1).wait_recv()

    def edge_drain(self, group):
        self.sum_all(group).wait_send()

        @pl.when(self.r < self.rows - 1)
        def _():
            self.halo_copy(group, 0).wait_send()

        @pl.when(self.r > 0)
        def _():
            self.halo_copy(group, 1).wait_send()


def block_kernel(head_dim, width, x_hbm, ln_hbm, wq_hbm, wk_hbm, wv_hbm, wo_hbm, gn_hbm, conv_hbm, bias_hbm,
                 out_ref, x_s, ln_s, gn_s, bias_s, w_s, conv_s, n_s, g_s, last_s, wkv_s, wo_s, q_s, k_s, v_s,
                 acc_s, top_s, att_s, u_s, all_s, halo_s, act_s, load, *sems):
    frames, own, channels = x_s.shape
    half = own // 2
    tiles = -(-HEADS // PER_TILE)
    wide = tiles * LANES
    used = PER_TILE * head_dim
    cut = (channels // LANES) * LANES
    scale = math.log2(math.e) / math.sqrt(head_dim)
    net = Net(g_s, last_s, u_s, all_s, halo_s, sems)
    lead = net.lead

    loads = [(x_hbm, x_s), (ln_hbm, ln_s), (wq_hbm, w_s.at[0]), (wk_hbm, w_s.at[1]),
             (wv_hbm, w_s.at[2]), (wo_hbm, w_s.at[3]), (gn_hbm, gn_s), (bias_hbm, bias_s),
             (conv_hbm, conv_s)]
    copies = [pltpu.make_async_copy(a, b, load.at[i]) for i, (a, b) in enumerate(loads)]
    for copy in copies:
        copy.start()
    net.hail()

    heads_in = [min(PER_TILE, HEADS - t * PER_TILE) for t in range(tiles)]
    lane = lax.broadcasted_iota(jnp.int32, (own, LANES), 1)
    low = one_hot(channels, 2 * channels, lambda i, j: i == j)
    high = one_hot(channels, 2 * channels, lambda i, j: i + channels == j)
    copies[0].wait()
    copies[1].wait()
    gain = ln_s[...].astype(F32).reshape(1, channels)

    def norm(f):
        normed = normalize(x_s[f], gain)
        n_s[f] = normed
        packed = (dot(normed[:half], low) + dot(normed[half:], high)).astype(BF)
        if f + 1 < frames:
            g_s[1 + f, net.c, net.z] = packed
        else:
            last_s[...] = packed
        if f == 0:
            @pl.when(net.b == 0)
            def _():
                g_s[0, net.c, net.z] = packed
                g_s[lead, net.c, net.z] = packed

    @pl.when(net.r == 0)
    def _():
        halo_s[0] = jnp.zeros(halo_s.shape[1:], BF)

    @pl.when(net.r == net.rows - 1)
    def _():
        halo_s[1] = jnp.zeros(halo_s.shape[1:], BF)

    norm(0)
    net.greet()
    net.spread_own(1)
    net.tree_step(0)
    norm(1)
    net.spread_own(2)
    norm(frames - 1)
    norm(2)
    net.prev_start()

    for i in range(2, 6):
        copies[i].wait()
    spread = one_hot(channels, wide,
                     lambda i, j: (j % LANES < used) & (i == (j // LANES) * used + j % LANES))
    wq = dot(w_s[0], spread).astype(BF)
    wkv_s[...] = jnp.zeros(wkv_s.shape, BF)
    for i in range(2):
        part = dot(w_s[1 + i], spread).astype(BF)
        wkv_s[0, :channels, i * wide:(i + 1) * wide] = part
        wkv_s[1, channels - cut:2 * channels - cut, i * wide:(i + 1) * wide] = part
    wo_s[...] = dot_tn(spread, w_s[3]).astype(BF)
    net.forward(1)
    net.spread_own(3)
    net.tree_step(1)
    net.cross_step()
    for f in range(frames):
        q = dot(n_s[f], wq)
        for t in range(tiles):
            part = q[:, t * LANES:(t + 1) * LANES]
            for j in range(heads_in[t]):
                kept = jnp.where((lane >= j * head_dim) & (lane < (j + 1) * head_dim), part, 0.0)
                q_s[f, t, j * own:(j + 1) * own, :] = kept.astype(BF)

    def project(slot):
        rows = g_s.shape[2] * half
        count = g_s.shape[1]
        inside = lax.broadcasted_iota(jnp.int32, (rows, wide), 1) % LANES
        for i in range(count):
            packed = g_s[slot, i].reshape(rows, 2 * channels)
            for side in range(2):
                view = packed[:, side * cut:side * cut + wide]
                both = dot(view, wkv_s[side])
                at = (2 * i + side) * rows
                k_s[at:at + rows, :] = both[:, :wide].astype(BF)
                v_s[at:at + rows, :] = jnp.where(inside >= used, 1.0, both[:, wide:]).astype(BF)

    def unit(f, t):
        rows = heads_in[t] * own
        s = dot_nt(q_s[f, t, :rows, :], k_s[:, t * LANES:(t + 1) * LANES])
        top = jnp.max(s, axis=-1, keepdims=True)
        w = jnp.exp2((s - top) * scale).astype(BF)
        return top, dot(w, v_s[:, t * LANES:(t + 1) * LANES]), rows

    def first(f, t):
        top, acc, rows = unit(f, t)
        acc_s[f, t, :rows, :] = acc
        top_s[f, t, :rows, :] = jnp.broadcast_to(top, (rows, LANES))

    def second(f, carry):
        for t in range(tiles):
            top, acc, rows = unit(f, t)
            before = top_s[f, t, :rows, :]
            most = jnp.maximum(before, top)
            acc = acc * jnp.exp2((top - most) * scale) + acc_s[f, t, :rows, :] * jnp.exp2((before - most) * scale)
            acc = acc / acc[:, used:used + 1]
            whole = jnp.zeros((own, LANES), F32)
            for j in range(heads_in[t]):
                whole = jnp.where((lane >= j * head_dim) & (lane < (j + 1) * head_dim),
                                  acc[j * own:(j + 1) * own, :], whole)
            att_s[:, t * LANES:(t + 1) * LANES] = whole.astype(BF)
        updated = (x_s[f].astype(F32) + dot(att_s[...], wo_s[...])).astype(BF)
        u_s[f] = updated
        wider = updated.astype(F32)
        all_s[0, f, 0:1, :] = jnp.sum(wider, axis=0, keepdims=True)
        all_s[0, f, 1:2, :] = jnp.sum(wider * wider, axis=0, keepdims=True)
        return carry

    net.forward(2)
    net.hand_over(1)
    net.tree_step(2)
    net.finish(1)
    net.tree_step(3)
    project(1)
    net.forward(3)
    first(1, 0)
    net.tree_step(4)
    net.hand_over(2)
    first(1, 1)
    net.lead_arrived()
    net.spread_own(lead)
    first(1, 2)
    net.finish(2)
    project(2)
    net.prev_arrived()
    net.spread_own(0)
    first(2, 0)
    net.hand_over(3)
    first(2, 1)
    net.forward(lead)
    first(2, 2)
    net.finish(3)
    project(3)
    first(3, 0)
    net.forward(0)
    first(3, 1)
    net.hand_over(lead)
    first(3, 2)
    net.finish(lead)
    project(lead)
    first(0, 0)
    first(0, 1)
    first(0, 2)

    def rest(f, carry):
        @pl.when(f == frames - 1)
        def _():
            net.hand_over(0)
        return second(f, carry)

    lax.fori_loop(1, frames, rest, 0)
    most, final = (1, frames - 1), (0, 1)
    net.edge_start(most)
    net.finish(0)
    project(0)
    second(0, 0)
    net.edge_start(final)

    for i in range(6, len(copies)):
        copies[i].wait()
    gn_gain = gn_s[...].astype(F32).reshape(1, channels)
    bias = bias_s[...].astype(F32).reshape(1, channels)
    group = channels // GROUPS
    same = (lax.broadcasted_iota(jnp.int32, (channels, channels), 0) // group
            == lax.broadcasted_iota(jnp.int32, (channels, channels), 1) // group)
    same = jnp.where(same, 1.0, 0.0)
    tall = own + 2 * width
    place = lax.broadcasted_iota(jnp.int32, (tall, channels), 0)
    column = place % width
    real = ((place >= width) | (net.r > 0)) & ((place < width + own) | (net.r < net.rows - 1))
    counted = own * net.rows * group

    def convolve(group):
        start, count = group
        net.edge_wait(group)
        for f in range(start, start + count):
            total = all_s[0, f]
            for d in range(1, net.rows):
                total = total + all_s[d, f]
            grouped = jnp.dot(jnp.concatenate([total] * 4, axis=0), same, preferred_element_type=F32,
                              precision=lax.Precision.HIGHEST)
            mean = grouped[0:1] / counted
            var = grouped[1:2] / counted - mean * mean
            u = jnp.concatenate([halo_s[0, f], u_s[f], halo_s[1, f]], axis=0).astype(F32)
            v = (u - mean) * lax.rsqrt(var + 1e-5) * gn_gain
            v = jnp.where(real, v / (1.0 + jnp.exp(-v)), 0.0)
            act_s[0, f] = jnp.where(column == 0, 0.0, pltpu.roll(v, 1, 0)).astype(BF)
            act_s[1, f] = v.astype(BF)
            act_s[2, f] = jnp.where(column == width - 1, 0.0, pltpu.roll(v, tall - 1, 0)).astype(BF)
        rows = count * own
        summed = u_s[start:start + count].reshape(rows, channels).astype(F32) + bias
        for a in range(3):
            for b in range(3):
                window = act_s[b, start:start + count, a * width:a * width + own, :].reshape(rows, channels)
                summed = summed + dot(window, conv_s[a, b])
        out_ref[start:start + count] = summed.astype(BF).reshape(count, own, channels)

    convolve(most)
    convolve(final)

    for s in range(lead + 1):
        net.drain(s)
    net.prev_drain()
    net.tree_drain()
    net.edge_drain(most)
    net.edge_drain(final)


def body(latents, ln_gain, q_weight, k_weight, v_weight, o_weight, gn_gain, conv_weight, conv_bias):
    frames, row_count, col_count, channels = latents.shape
    own = row_count * col_count
    head_dim = channels // HEADS
    tiles = -(-HEADS // PER_TILE)
    wide = tiles * LANES
    rows = lax.axis_size("row")
    slots = frames + 1
    keys = rows * own
    hbm = pl.BlockSpec(memory_space=pl.ANY)
    dma = pltpu.SemaphoreType.DMA
    out = pl.pallas_call(
        functools.partial(block_kernel, head_dim, col_count),
        out_shape=jax.ShapeDtypeStruct((frames, own, channels), BF),
        in_specs=[hbm] * 9,
        out_specs=pl.BlockSpec(memory_space=pltpu.VMEM),
        scratch_shapes=[
            pltpu.VMEM((frames, own, channels), BF),
            pltpu.VMEM((channels,), BF),
            pltpu.VMEM((channels,), BF),
            pltpu.VMEM((channels,), BF),
            pltpu.VMEM((4, channels, channels), BF),
            pltpu.VMEM((3, 3, channels, channels), BF),
            pltpu.VMEM((frames, own, channels), BF),
            pltpu.VMEM((slots, 2, rows // 2, own // 2, 2 * channels), BF),
            pltpu.VMEM((own // 2, 2 * channels), BF),
            pltpu.VMEM((2, wide, 2 * wide), BF),
            pltpu.VMEM((wide, channels), BF),
            pltpu.VMEM((frames, tiles, PER_TILE * own, LANES), BF),
            pltpu.VMEM((keys, wide), BF),
            pltpu.VMEM((keys, wide), BF),
            pltpu.VMEM((frames, tiles, PER_TILE * own, LANES), F32),
            pltpu.VMEM((frames, tiles, PER_TILE * own, LANES), F32),
            pltpu.VMEM((own, wide), BF),
            pltpu.VMEM((frames, own, channels), BF),
            pltpu.VMEM((rows, frames, 2, channels), F32),
            pltpu.VMEM((2, frames, col_count, channels), BF),
            pltpu.VMEM((3, frames, own + 2 * col_count, channels), BF),
            dma((9,)),
            dma((slots, 4)),
            dma((slots,)),
            dma((TREE_CHILDREN,)),
            dma,
            pltpu.SemaphoreType.REGULAR((TREE_CHILDREN,)),
            pltpu.SemaphoreType.REGULAR,
            dma((frames,)),
            dma((frames,)),
            dma((frames, 2)),
            dma((frames, 2)),
        ],
        compiler_params=pltpu.CompilerParams(
            collective_id=0, has_side_effects=True, vmem_limit_bytes=56 * 1024 * 1024),
    )(latents.reshape(frames, own, channels), ln_gain, q_weight, k_weight, v_weight,
      o_weight, gn_gain, conv_weight, conv_bias)
    return out.reshape(frames, row_count, col_count, channels)


def solution(mesh):
    in_specs = (P("frame", "row", None, None), P(), P(), P(), P(), P(), P(), P(), P())
    out_specs = P("frame", "row", None, None)
    return jax.shard_map(body, mesh=mesh, in_specs=in_specs, out_specs=out_specs, check_vma=False)
```
